32 devices in a mesh: row: 8 (over z, x), col: 4 (over y, core).
Axes of the slice: x: 2, y: 2, z: 4, core: 2. Of those that a mesh axis runs over, the one named last changes fastest.
Arguments:
- panel: float32 [128, 131072], P('col', 'row'), may hold values from -6 to 6
- signs: int32 [131072], P('row'), may hold values from -1 to 1, as said below
- offsets: int32 [8192], P('row'), may hold values from 0 to 16383
- owners: int32 [8192, 1], P('row'), may hold values from 0 to 7; in each aligned block of 1024 rows (0 to 1023, 1024 to 2047, ...) at most 256 rows name the same one
Outputs:
- grams: float32 [8, 128, 128], P('row', 'col')
The draws below stay inside these ranges and needn't reach their ends.
Inputs may be any that keep to these rules, and one draw needn't show every extreme that they name: `signs`: each entry is +1 or -1. `owners`: in each aligned block of 1024 samples (the list of one source), no owner is named more than 256 times, a bound that some block reaches; every owner is named somewhere.
All inputs are finite; a program needn't handle non-finite values.
Results may differ from the reference program's by a relative error of at most 0.0003.
Values sent between devices are 32-bit elements; how exact they have to be, the bound alone decides.
No kernel may reach another device: no remote copies, remote signals or barrier semaphores. Data moves between devices by JAX's collectives and lax.ppermute only.
A program may use at most 128 MiB of HBM per device.

```python
import math
import jax
import jax.numpy as jnp
import numpy as np
from jax import lax

C = 128
ROWS_DEV = 16384
KDEV = 1024
ROWS = 131072
SAMPLES = 8192
OWNERS = 8
CAP = 256
N_ROW = 8


def draw_signs(key, part):
    return 2 * jax.random.randint(key, (ROWS,), 0, 2, dtype=jnp.int32) - 1


def plant(drawn, rng, low, high):
    longest = drawn.shape.index(max(drawn.shape))
    spots = []
    for shift in (0, 1):
        where = [jax.random.randint(jax.random.fold_in(rng, axis), (), 0, length) for axis, length in enumerate(drawn.shape)]
        where[longest] = (where[longest] + shift) % drawn.shape[longest]
        spots.append(tuple(where))
    return drawn.at[spots[0]].set(low).at[spots[1]].set(high)


def block_levels(key, extent, pieces, low, top_value):
    def one(axis_at, shards_of):
        heights = jax.random.uniform(jax.random.fold_in(jax.random.fold_in(key, 6), axis_at), (shards_of,), jnp.float32, low / len(pieces), top_value / len(pieces))
        return jnp.repeat(jnp.exp(heights), extent[axis_at] // shards_of).reshape((-1,) + (1,) * (len(extent) - axis_at - 1))

    loudness = one(*pieces[0])
    for cut in pieces[1:]:
        loudness = loudness * one(*cut)
    return loudness


def assign_block(own_key, own, number, rows, amount, top, limit, lean):
    order = jax.random.permutation(own_key, amount)
    packed, usual = shares(amount, rows * top, limit, lean, True), shares(amount, rows * top, limit, lean, False)
    places = jnp.arange(amount)

    def named(tallies, rotation):
        used = int((tallies > 0).sum())
        fixed = max(1, used // 4)
        shifted = fixed + (places - fixed + rotation * (used - fixed)) % max(1, amount - fixed)
        return jnp.zeros((amount,), jnp.int32).at[order[jnp.where(places < fixed, places, shifted)]].set(jnp.asarray(tallies, jnp.int32))

    tallies = jnp.where(number % 4 == 0, named(packed, number // 4), named(usual, number - number // 4 - 1))
    mixed = jax.random.permutation(jax.random.fold_in(own, 3), amount)
    source_of, sink = mixed[0:amount // 2 * 2:2], mixed[1:amount // 2 * 2:2]
    room = jnp.minimum(tallies[source_of] - 1, limit - tallies[sink]) // 2
    room = jnp.where((source_of == order[0]) | (sink == order[0]) | (tallies[sink] == 0), 0, jnp.maximum(room, 0))
    shifted = jax.random.randint(jax.random.fold_in(own, 4), (amount // 2,), 0, 1 << 20) % (room + 1)
    tallies = tallies.at[source_of].add(-shifted).at[sink].add(shifted)
    items = jnp.searchsorted(jnp.cumsum(tallies), jnp.arange(rows * top), side="right").astype(jnp.int32)
    grid = items.reshape(top, rows).T
    grid = grid[jax.random.permutation(jax.random.fold_in(own, 1), rows)]
    rotation = jax.random.randint(jax.random.fold_in(own, 2), (rows, 1), 0, top)
    return jnp.take_along_axis(grid, (jnp.arange(top)[None, :] + rotation) % top, axis=1)


def shares(amount, total, reach, lean, full):
    portions = [(1 << 20) // math.isqrt(rank ** lean) + 1 for rank in range(1, amount + 1)]
    largest = reach if full else min(reach, max(-(-total // amount), total * portions[0] // sum(portions)))
    least = 1 if total - largest >= amount - 1 else 0
    counts, surplus = [largest] + [least] * (amount - 1), total - largest - least * (amount - 1)
    while surplus > 0:
        free = [i for i in range(1, amount) if counts[i] < largest] or [i for i in range(1, amount) if counts[i] < reach]
        pool, budget = sum([portions[i] for i in free]), surplus
        for i in free:
            addition = min(reach - counts[i], max(1, budget * portions[i] // pool), surplus)
            counts[i] = counts[i] + addition
            surplus = surplus - addition
    return np.array(counts)


def gaussian(key, dims, scale, reach, cuts=(), kind=jnp.bfloat16):
    level = block_levels(key, dims, cuts, -0.22, 0.18) if cuts else 1.0
    entries = jax.random.normal(key, dims, jnp.float32) * scale * level
    return jnp.minimum(jnp.maximum(entries, -reach), reach).astype(kind)


def setup_inputs(seed: int = 0) -> dict:
    keys = jax.random.split(jax.random.key(seed), 5)
    panel = gaussian(keys[0], (C, ROWS), 1.0, 6.0, ((0, 4), (1, 8)), jnp.float32)
    signs = draw_signs(jax.random.fold_in(keys[4], 71), 0)
    offsets = plant(jax.random.randint(keys[2], (SAMPLES,), 0, ROWS_DEV), jax.random.fold_in(keys[2], 1), 0, ROWS_DEV - 1).astype(jnp.int32)
    owners_keys = jax.random.split(jax.random.fold_in(keys[3], 1), SAMPLES // KDEV)
    owners_turns = jax.random.permutation(jax.random.fold_in(keys[3], 3), SAMPLES // KDEV)
    owners = jax.vmap(lambda own, number: assign_block(jax.random.fold_in(keys[3], 2), own, number, KDEV, OWNERS, 1, CAP, 2))(owners_keys, owners_turns).reshape((SAMPLES, 1))
    return dict(panel=panel, signs=signs, offsets=offsets, owners=owners)


def sylvester(order):
    index = jnp.arange(order, dtype=jnp.int32)
    common = jnp.bitwise_and(index[:, None], index[None, :])
    parity = jnp.zeros((order, order), jnp.int32)
    for level in range(max(order.bit_length() - 1, 0)):
        parity = parity + jnp.bitwise_and(jnp.right_shift(common, level), 1)
    return (1 - 2 * (parity % 2)).astype(jnp.float32)

def reference(panel, signs, offsets, owners):
    devices = N_ROW
    blocks = ROWS_DEV // 128
    table_a = sylvester(128)
    table_b = sylvester(blocks)
    table_p = sylvester(devices)
    scale = 1.0 / jnp.sqrt(jnp.float32(ROWS))
    source = jnp.arange(SAMPLES, dtype=jnp.int32) // KDEV
    mixing = table_p[source]
    sign_rows = signs.astype(jnp.float32).reshape(devices, 128, blocks)
    high = lax.Precision.HIGHEST

    def one_block(columns):
        signed = columns.reshape(-1, devices, 128, blocks) * sign_rows
        inner = jnp.einsum('cqab,bd->cqad', signed, table_b, precision=high)
        outer = jnp.einsum('ea,cqad->cqed', table_a, inner, precision=high)
        outer = outer.reshape(-1, devices, ROWS_DEV)
        picked = outer[:, :, offsets]
        return jnp.einsum('cqk,kq->ck', picked, mixing, precision=high) * scale
    sketch = lax.map(one_block, panel.reshape(C // 16, 16, ROWS)).reshape(C, SAMPLES)
    owner_ids = owners[:, 0]

    def one_owner(owner):
        weight = (owner_ids == owner).astype(jnp.float32)
        return jnp.einsum('ck,dk->cd', sketch * weight[None, :], sketch, precision=high) / KDEV
    return lax.map(one_owner, jnp.arange(OWNERS, dtype=jnp.int32))
```

```python
import functools

import jax
import jax.numpy as jnp
from jax import lax
from jax.experimental import pallas as pl
from jax.experimental.pallas import tpu as pltpu
from jax.sharding import PartitionSpec as P

LANES = 128
f32, bf16 = jnp.float32, jnp.bfloat16


def swapped(x, axis, distance):
    return lax.ppermute(x, axis, [(i, i ^ distance) for i in range(lax.axis_size(axis))])


def parity(v):
    v = v ^ (v >> 8)
    v = v ^ (v >> 4)
    v = v ^ (v >> 2)
    v = v ^ (v >> 1)
    return v & 1


def butterflies(values):
    step = 1
    while step < len(values):
        out = list(values)
        for i in range(len(values)):
            if not i & step:
                out[i] = values[i] + values[i | step]
                out[i | step] = values[i] - values[i | step]
        values = out
        step *= 2
    return values


def halves(x):
    top = x.astype(bf16)
    return top, (x - top.astype(f32)).astype(bf16)


def wht_kernel(width, x_ref, sign_ref, table_ref, work_ref):
    group = LANES // width
    bands = width // 8

    def first(lo, _):
        signs = [sign_ref[pl.ds(hi * 8 + lo, 1), :].astype(f32) for hi in range(16)]
        for band in range(bands):
            values = [
                x_ref[pl.ds(band * 8, 8), pl.ds(pl.multiple_of((hi * 8 + lo) * LANES, LANES), LANES)] * signs[hi]
                for hi in range(16)
            ]
            for hi, value in enumerate(butterflies(values)):
                work_ref[hi * 8 + lo, pl.ds(band * 8, 8), :] = value
        return 0

    lax.fori_loop(0, 8, first, 0)
    row = lax.broadcasted_iota(jnp.int32, (LANES, 2 * LANES), 0)
    column = lax.broadcasted_iota(jnp.int32, (LANES, 2 * LANES), 1)
    hadamard = (1 - 2 * parity(row & (column & (LANES - 1)))).astype(f32).astype(bf16)
    lane = lax.broadcasted_iota(jnp.int32, (8, LANES), 1) & (width - 1)

    def second(hi, _):
        rows = [
            butterflies([work_ref[hi * 8 + lo, pl.ds(band * 8, 8), :] for lo in range(8)]) for band in range(bands)
        ]
        y = jnp.concatenate([rows[band][lo] for lo in range(8) for band in range(bands)], axis=0)
        both = jnp.concatenate(halves(y), axis=1)
        mixed = lax.dot_general(hadamard, both, (((1,), (1,)), ((), ())), preferred_element_type=f32)
        for lo in range(8):
            block, place = divmod(lo, group)
            start = pl.multiple_of((hi * 8 + lo) * LANES, LANES)
            for r in range(0, LANES, 8):
                piece = mixed[r : r + 8, block * LANES : (block + 1) * LANES]
                table_ref[pl.ds(start + r, 8), :] = jnp.take_along_axis(piece, lane + place * width, axis=1)
        return 0

    lax.fori_loop(0, 16, second, 0)


def pick_kernel(width, slots, count, sources, unroll, offset_ref, table_ref, out_ref):
    group = LANES // width
    per = count // group
    lane = lax.broadcasted_iota(jnp.int32, (8, LANES), 1) // width
    sub = lax.broadcasted_iota(jnp.int32, (8, LANES), 0)
    me = lax.axis_index("row")
    for place, slot in enumerate(slots):
        sign = (1 - 2 * parity(me & (me ^ slot))).astype(f32)
        base = sources[place] * count

        def step(it, _):
            for u in range(unroll):
                inner = (it * unroll + u) * 8
                total = None
                for g in range(group):
                    for s in range(8):
                        spot = offset_ref[base + inner + (g * per + s)]
                        value = jnp.broadcast_to(table_ref[pl.ds(spot, 1), :], (8, LANES))
                        total = value if total is None else jnp.where((lane == g) & (sub == s), value, total)
                out_ref[pl.ds(pl.multiple_of(place * per + inner, 8), 8), :] = total * sign
            return 0

        lax.fori_loop(0, per // 8 // unroll, step, 0)


def gram_kernel(width, count, named, scale, owner_ref, *refs):
    group = LANES // width
    per = count // group
    packed, out_ref = refs[:-1], refs[-1]
    lane = lax.broadcasted_iota(jnp.int32, (per, LANES), 1)
    parts, repeated = [], []
    for g in range(group):
        total = packed[g][...]
        for u in range(group):
            if u != g:
                moved = jnp.take_along_axis(packed[u][...], lane ^ ((u ^ g) * width), axis=1)
                total = jnp.where(lane // width == u, moved, total)
        parts.append(total)
        repeated.append(jnp.take_along_axis(packed[0][...], (lane & (width - 1)) + g * width, axis=1))
    sketch = jnp.concatenate(parts, axis=0)
    mine = jnp.concatenate(repeated, axis=0)
    top, low = halves(sketch)
    mine_top, mine_low = halves(mine)
    whose = jnp.broadcast_to(owner_ref[...], (count, LANES))
    tall = lax.broadcasted_iota(jnp.int32, (count, LANES), 1) // width
    zero = jnp.zeros((count, LANES), bf16)
    me, col = lax.axis_index("row"), lax.axis_index("col")
    turned = lax.broadcasted_iota(jnp.int32, (LANES, LANES), 1) ^ (col * width)
    over = (((0,), (0,)), ((), ()))
    bits = named.bit_length() - 1
    for block in range(named * width // LANES):
        match = whose == tall + block * group
        left = jnp.where(match, mine_top, zero)
        gram = lax.dot_general(left, top, over, preferred_element_type=f32)
        gram = gram + lax.dot_general(left, low, over, preferred_element_type=f32)
        left = jnp.where(match, mine_low, zero)
        gram = gram + lax.dot_general(left, top, over, preferred_element_type=f32)
        gram = jnp.take_along_axis(gram, turned, axis=1) * scale
        for k in range(group):
            slot = (block * group + k) ^ me
            place = 0
            for bit in range(bits):
                place = place | ((slot >> bit) & 1) << (bits - 1 - bit)
            out_ref[pl.ds(pl.multiple_of(place * width, 8), width), :] = gram[k * width : (k + 1) * width]


VMEM = pl.BlockSpec(memory_space=pltpu.VMEM)
SMEM = pl.BlockSpec(memory_space=pltpu.SMEM)


def reverse(i, bits):
    return int(format(i, f"0{bits}b")[::-1], 2) if bits else 0


def body(panel, signs, offsets, owners):
    width, row_count = panel.shape
    devices = lax.axis_size("row")
    bits = devices.bit_length() - 1
    count = offsets.shape[0]
    group = LANES // width
    per = count // group
    table = pl.pallas_call(
        functools.partial(wht_kernel, width),
        out_shape=jax.ShapeDtypeStruct((row_count, LANES), f32),
        in_specs=[VMEM] * 2,
        out_specs=VMEM,
        scratch_shapes=[pltpu.VMEM((LANES, width, LANES), f32)],
        name="wht",
    )(panel, signs.reshape(LANES, LANES))
    listed = offsets.reshape(count // LANES, LANES)
    for level in reversed(range(bits)):
        listed = jnp.concatenate([listed, swapped(listed, "row", 1 << level)], axis=0)
    listed = listed.reshape(-1)

    def pick(places):
        return pl.pallas_call(
            functools.partial(
                pick_kernel, width, [reverse(i, bits) for i in places], count, list(range(len(places))), 2
            ),
            out_shape=jax.ShapeDtypeStruct((len(places) * per, LANES), f32),
            in_specs=[SMEM, VMEM],
            out_specs=VMEM,
            name="pick",
        )(listed[places[0] * count : (places[-1] + 1) * count], table)

    half = devices // 2
    sent = pick(range(half, devices))
    kept = pick(range(half))
    arrived = swapped(sent, "row", 1)
    total = kept + arrived
    for level in range(1, bits):
        middle = total.shape[0] // 2
        total = total[:middle] + swapped(total[middle:], "row", 1 << level)
    packed = [total]
    col_bits = lax.axis_size("col").bit_length() - 1
    stacked = total[None]
    for level in reversed(range(col_bits)):
        stacked = jnp.concatenate([stacked, swapped(stacked, "col", 1 << level)], axis=0)
    packed = [stacked[reverse(u, col_bits)] for u in range(group)]
    scale = 1.0 / (devices * row_count * count)
    named = devices
    gram = pl.pallas_call(
        functools.partial(gram_kernel, width, count, named, scale),
        out_shape=jax.ShapeDtypeStruct((named * width, LANES), f32),
        in_specs=[VMEM] * (1 + group),
        out_specs=VMEM,
        name="gram",
    )(owners, *packed)
    for level in range(bits):
        middle = gram.shape[0] // 2
        gram = gram[:middle] + swapped(gram[middle:], "row", 1 << level)
    return gram[None]


def solution(mesh):
    placed = (P("col", "row"), P("row"), P("row"), P("row", None))
    return jax.shard_map(
        body, mesh=mesh, in_specs=placed, out_specs=P("row", "col", None), check_vma=False
    )
```

```python
import functools

import jax
import jax.numpy as jnp
from jax import lax
from jax.experimental import pallas as pl
from jax.experimental.pallas import tpu as pltpu
from jax.sharding import PartitionSpec as P

LANES = 128
f32, bf16 = jnp.float32, jnp.bfloat16


def swapped(x, axis, distance):
    return lax.ppermute(x, axis, [(i, i ^ distance) for i in range(lax.axis_size(axis))])


def parity(v):
    v = v ^ (v >> 8)
    v = v ^ (v >> 4)
    v = v ^ (v >> 2)
    v = v ^ (v >> 1)
    return v & 1


def butterflies(values):
    step = 1
    while step < len(values):
        out = list(values)
        for i in range(len(values)):
            if not i & step:
                out[i] = values[i] + values[i | step]
                out[i | step] = values[i] - values[i | step]
        values = out
        step *= 2
    return values


def halves(x):
    top = x.astype(bf16)
    return top, (x - top.astype(f32)).astype(bf16)


def wht_kernel(width, x_ref, sign_ref, table_ref, work_ref):
    group = LANES // width
    bands = width // 8

    def first(lo, _):
        signs = [sign_ref[pl.ds(hi * 8 + lo, 1), :].astype(f32) for hi in range(16)]
        for band in range(bands):
            values = [
                x_ref[pl.ds(band * 8, 8), pl.ds(pl.multiple_of((hi * 8 + lo) * LANES, LANES), LANES)] * signs[hi]
                for hi in range(16)
            ]
            for hi, value in enumerate(butterflies(values)):
                work_ref[hi * 8 + lo, pl.ds(band * 8, 8), :] = value
        return 0

    lax.fori_loop(0, 8, first, 0)
    row = lax.broadcasted_iota(jnp.int32, (LANES, 2 * LANES), 0)
    column = lax.broadcasted_iota(jnp.int32, (LANES, 2 * LANES), 1)
    hadamard = (1 - 2 * parity(row & (column & (LANES - 1)))).astype(f32).astype(bf16)
    lane = lax.broadcasted_iota(jnp.int32, (8, LANES), 1) & (width - 1)

    def second(hi, _):
        rows = [
            butterflies([work_ref[hi * 8 + lo, pl.ds(band * 8, 8), :] for lo in range(8)]) for band in range(bands)
        ]
        y = jnp.concatenate([rows[band][lo] for lo in range(8) for band in range(bands)], axis=0)
        both = jnp.concatenate(halves(y), axis=1)
        mixed = lax.dot_general(hadamard, both, (((1,), (1,)), ((), ())), preferred_element_type=f32)
        for lo in range(8):
            block, place = divmod(lo, group)
            start = pl.multiple_of((hi * 8 + lo) * LANES, LANES)
            for r in range(0, LANES, 8):
                piece = mixed[r : r + 8, block * LANES : (block + 1) * LANES]
                table_ref[pl.ds(start + r, 8), :] = jnp.take_along_axis(piece, lane + place * width, axis=1)
        return 0

    lax.fori_loop(0, 16, second, 0)


def pick_kernel(width, slots, count, sources, unroll, offset_ref, table_ref, out_ref):
    group = LANES // width
    per = count // group
    lane = lax.broadcasted_iota(jnp.int32, (8, LANES), 1) // width
    sub = lax.broadcasted_iota(jnp.int32, (8, LANES), 0)
    me = lax.axis_index("row")
    for place, slot in enumerate(slots):
        sign = (1 - 2 * parity(me & (me ^ slot))).astype(f32)
        base = sources[place] * count

        def step(it, _):
            for u in range(unroll):
                inner = (it * unroll + u) * 8
                total = None
                for g in range(group):
                    for s in range(8):
                        spot = offset_ref[base + inner + (g * per + s)]
                        value = jnp.broadcast_to(table_ref[pl.ds(spot, 1), :], (8, LANES))
                        total = value if total is None else jnp.where((lane == g) & (sub == s), value, total)
                out_ref[pl.ds(pl.multiple_of(place * per + inner, 8), 8), :] = total * sign
            return 0

        lax.fori_loop(0, per // 8 // unroll, step, 0)


def gram_kernel(width, count, named, scale, owner_ref, *refs):
    group = LANES // width
    per = count // group
    packed, out_ref = refs[:-1], refs[-1]
    lane = lax.broadcasted_iota(jnp.int32, (per, LANES), 1)
    parts, repeated = [], []
    for g in range(group):
        total = packed[g][...]
        for u in range(group):
            if u != g:
                moved = jnp.take_along_axis(packed[u][...], lane ^ ((u ^ g) * width), axis=1)
                total = jnp.where(lane // width == u, moved, total)
        parts.append(total)
        repeated.append(jnp.take_along_axis(packed[0][...], (lane & (width - 1)) + g * width, axis=1))
    sketch = jnp.concatenate(parts, axis=0)
    mine = jnp.concatenate(repeated, axis=0)
    top, low = halves(sketch)
    mine_top, mine_low = halves(mine)
    whose = jnp.broadcast_to(owner_ref[...], (count, LANES))
    tall = lax.broadcasted_iota(jnp.int32, (count, LANES), 1) // width
    zero = jnp.zeros((count, LANES), bf16)
    me, col = lax.axis_index("row"), lax.axis_index("col")
    turned = lax.broadcasted_iota(jnp.int32, (LANES, LANES), 1) ^ (col * width)
    over = (((0,), (0,)), ((), ()))
    bits = named.bit_length() - 1
    for block in range(named * width // LANES):
        match = whose == tall + block * group
        left = jnp.where(match, mine_top, zero)
        gram = lax.dot_general(left, top, over, preferred_element_type=f32)
        gram = gram + lax.dot_general(left, low, over, preferred_element_type=f32)
        left = jnp.where(match, mine_low, zero)
        gram = gram + lax.dot_general(left, top, over, preferred_element_type=f32)
        gram = jnp.take_along_axis(gram, turned, axis=1) * scale
        for k in range(group):
            slot = (block * group + k) ^ me
            place = 0
            for bit in range(bits):
                place = place | ((slot >> bit) & 1) << (bits - 1 - bit)
            out_ref[pl.ds(pl.multiple_of(place * width, 8), width), :] = gram[k * width : (k + 1) * width]


VMEM = pl.BlockSpec(memory_space=pltpu.VMEM)
SMEM = pl.BlockSpec(memory_space=pltpu.SMEM)


def reverse(i, bits):
    return int(format(i, f"0{bits}b")[::-1], 2) if bits else 0


def body(panel, signs, offsets, owners):
    width, row_count = panel.shape
    devices = lax.axis_size("row")
    bits = devices.bit_length() - 1
    count = offsets.shape[0]
    group = LANES // width
    per = count // group
    table = pl.pallas_call(
        functools.partial(wht_kernel, width),
        out_shape=jax.ShapeDtypeStruct((row_count, LANES), f32),
        in_specs=[VMEM] * 2,
        out_specs=VMEM,
        scratch_shapes=[pltpu.VMEM((LANES, width, LANES), f32)],
        name="wht", compiler_params=pltpu.CompilerParams(vmem_limit_bytes=24 << 20),
    )(panel, signs.reshape(LANES, LANES))
    listed = offsets.reshape(count // LANES, LANES)
    for level in reversed(range(bits)):
        listed = jnp.concatenate([listed, swapped(listed, "row", 1 << level)], axis=0)
    listed = listed.reshape(-1)

    def pick(places):
        return pl.pallas_call(
            functools.partial(
                pick_kernel, width, [reverse(i, bits) for i in places], count, list(range(len(places))), 2
            ),
            out_shape=jax.ShapeDtypeStruct((len(places) * per, LANES), f32),
            in_specs=[SMEM, VMEM],
            out_specs=VMEM,
            name="pick", compiler_params=pltpu.CompilerParams(vmem_limit_bytes=24 << 20),
        )(listed[places[0] * count : (places[-1] + 1) * count], table)

    half = devices // 2
    sent = pick(range(half, devices))
    kept = pick(range(half))
    arrived = swapped(sent, "row", 1)
    total = kept + arrived
    for level in range(1, bits):
        middle = total.shape[0] // 2
        total = total[:middle] + swapped(total[middle:], "row", 1 << level)
    packed = [total]
    col_bits = lax.axis_size("col").bit_length() - 1
    stacked = total[None]
    for level in reversed(range(col_bits)):
        stacked = jnp.concatenate([stacked, swapped(stacked, "col", 1 << level)], axis=0)
    packed = [stacked[reverse(u, col_bits)] for u in range(group)]
    scale = 1.0 / (devices * row_count * count)
    named = devices
    gram = pl.pallas_call(
        functools.partial(gram_kernel, width, count, named, scale),
        out_shape=jax.ShapeDtypeStruct((named * width, LANES), f32),
        in_specs=[VMEM] * (1 + group),
        out_specs=VMEM,
        name="gram", compiler_params=pltpu.CompilerParams(vmem_limit_bytes=24 << 20),
    )(owners, *packed)
    for level in range(bits):
        middle = gram.shape[0] // 2
        gram = gram[:middle] + swapped(gram[middle:], "row", 1 << level)
    return gram[None]


def solution(mesh):
    placed = (P("col", "row"), P("row"), P("row"), P("row", None))
    return jax.shard_map(
        body, mesh=mesh, in_specs=placed, out_specs=P("row", "col", None), check_vma=False
    )
```

```python
import functools

import jax
import jax.numpy as jnp
from jax import lax
from jax.experimental import pallas as pl
from jax.experimental.pallas import tpu as pltpu
from jax.sharding import PartitionSpec as P


LANES = 128
f32, bf16 = jnp.float32, jnp.bfloat16


def swapped(x, axis, distance):
    return lax.ppermute(x, axis, [(i, i ^ distance) for i in range(lax.axis_size(axis))])


def parity(v):
    v = v ^ (v >> 8)
    v = v ^ (v >> 4)
    v = v ^ (v >> 2)
    v = v ^ (v >> 1)
    return v & 1


def butterflies(values):
    step = 1
    while step < len(values):
        out = list(values)
        for i in range(len(values)):
            if not i & step:
                out[i] = values[i] + values[i | step]
                out[i | step] = values[i] - values[i | step]
        values = out
        step *= 2
    return values


def halves(x):
    top = x.astype(bf16)
    return top, (x - top.astype(f32)).astype(bf16)


def rows_kernel(width, x_ref, sign_ref, work_ref):
    def some(lo, _):
        signs = [sign_ref[pl.ds(hi * 8 + lo, 1), :].astype(f32) for hi in range(16)]
        for band in range(width // 8):
            rows = pl.ds(band * 8, 8)
            values = []
            for hi in range(16):
                start = pl.multiple_of((hi * 8 + lo) * LANES, LANES)
                values.append(x_ref[rows, pl.ds(start, LANES)] * signs[hi])
            for hi, value in enumerate(butterflies(values)):
                work_ref[hi * 8 + lo, rows, :] = value
        return 0

    lax.fori_loop(0, 8, some, 0)


def table_kernel(width, work_ref, table_ref):
    group = LANES // width
    bands = width // 8
    pair = 2 if width * 8 >= 2 * width else 1
    row = lax.broadcasted_iota(jnp.int32, (LANES, 2 * LANES), 0)
    column = lax.broadcasted_iota(jnp.int32, (LANES, 2 * LANES), 1)
    hadamard = (1 - 2 * parity(row & (column & (LANES - 1)))).astype(f32).astype(bf16)

    def some(hi, _):
        rows = [
            butterflies([work_ref[hi * 8 + lo, pl.ds(band * 8, 8), :] for lo in range(8)]) for band in range(bands)
        ]
        y = jnp.concatenate([rows[band][lo] for lo in range(8) for band in range(bands)], axis=0)
        top, low = halves(y)
        for e in range(0, 8, pair):
            both = [
                jnp.concatenate([v[(e + i) * width : (e + i + 1) * width] for i in range(pair) for _ in range(group)])
                for v in (top, low)
            ]
            mixed = lax.dot_general(
                hadamard,
                jnp.concatenate(both, axis=1),
                (((1,), (1,)), ((), ())),
                preferred_element_type=f32,
            )
            for i in range(pair):
                start = pl.multiple_of((hi * 8 + e + i) * LANES, LANES)
                table_ref[pl.ds(start, LANES), :] = mixed[:, i * LANES : (i + 1) * LANES]
        return 0

    lax.fori_loop(0, 16, some, 0, unroll=4)


def pick_kernel(width, slots, count, straight, *refs):
    offset_refs, table_ref, out_ref = refs[:-2], refs[-2], refs[-1]
    group = LANES // width
    per = count // group
    lane = lax.broadcasted_iota(jnp.int32, (8, LANES), 1) // width
    sub = lax.broadcasted_iota(jnp.int32, (8, LANES), 0)
    in_sub = [sub == s for s in range(8)]
    in_lane = [lane == g for g in range(group)]
    me = lax.axis_index("row")
    for place, slot in enumerate(slots):
        sign = (1 - 2 * parity(me & (me ^ slot))).astype(f32)

        def block(inner):
            total = None
            for g in range(group):
                part = None
                for s in range(8):
                    spot = offset_refs[place][inner + (g * per + s)]
                    value = jnp.broadcast_to(table_ref[pl.ds(spot, 1), :], (8, LANES))
                    part = value if part is None else jnp.where(in_sub[s], value, part)
                total = part if total is None else jnp.where(in_lane[g], part, total)
            return total * sign

        if straight:
            for inner in range(0, per, 8):
                out_ref[pl.ds(place * per + inner, 8), :] = block(inner)
        else:

            def some(it, _):
                inner = pl.multiple_of(it * 8, 8)
                out_ref[pl.ds(place * per + inner, 8), :] = block(inner)
                return 0

            lax.fori_loop(0, per // 8, some, 0)


def gram_kernel(width, count, named, scale, owner_ref, *refs):
    group = LANES // width
    per = count // group
    packed, out_ref = refs[:-1], refs[-1]
    lane = lax.broadcasted_iota(jnp.int32, (per, LANES), 1)
    parts, repeated = [], []
    for g in range(group):
        total = packed[g][...]
        for u in range(group):
            if u != g:
                moved = jnp.take_along_axis(packed[u][...], lane ^ ((u ^ g) * width), axis=1)
                total = jnp.where(lane // width == u, moved, total)
        parts.append(total)
        repeated.append(jnp.take_along_axis(packed[0][...], (lane & (width - 1)) + g * width, axis=1))
    sketch = jnp.concatenate(parts, axis=0)
    mine = jnp.concatenate(repeated, axis=0)
    top, low = halves(sketch)
    mine_top, mine_low = halves(mine)
    whose = jnp.broadcast_to(owner_ref[...], (count, LANES))
    tall = lax.broadcasted_iota(jnp.int32, (count, LANES), 1) // width
    zero = jnp.zeros((count, LANES), bf16)
    me, col = lax.axis_index("row"), lax.axis_index("col")
    turned = lax.broadcasted_iota(jnp.int32, (LANES, LANES), 1) ^ (col * width)
    over = (((0,), (0,)), ((), ()))
    for block in range(named * width // LANES):
        match = whose == tall + block * group
        left = jnp.where(match, mine_top, zero)
        gram = lax.dot_general(left, top, over, preferred_element_type=f32)
        gram = gram + lax.dot_general(left, low, over, preferred_element_type=f32)
        left = jnp.where(match, mine_low, zero)
        gram = gram + lax.dot_general(left, top, over, preferred_element_type=f32)
        gram = jnp.take_along_axis(gram, turned, axis=1) * scale
        for k in range(group):
            slot = (block * group + k) ^ me
            place = (slot & 3) * (named // 4) + (slot >> 2)
            out_ref[pl.ds(pl.multiple_of(place * width, 8), width), :] = gram[k * width : (k + 1) * width]


VMEM = pl.BlockSpec(memory_space=pltpu.VMEM)
SMEM = pl.BlockSpec(memory_space=pltpu.SMEM)
PARAMS = pltpu.CompilerParams(vmem_limit_bytes=24 << 20)


def transform_rows(panel, signs):
    width, _ = panel.shape
    return pl.pallas_call(
        functools.partial(rows_kernel, width),
        out_shape=jax.ShapeDtypeStruct((LANES, width, LANES), f32),
        in_specs=[VMEM] * 2,
        out_specs=VMEM,
        compiler_params=PARAMS,
        name="rows",
    )(panel, signs.reshape(LANES, LANES))


def transform_table(work, width):
    return pl.pallas_call(
        functools.partial(table_kernel, width),
        out_shape=jax.ShapeDtypeStruct((LANES * LANES, LANES), f32),
        in_specs=[VMEM],
        out_specs=VMEM,
        compiler_params=PARAMS,
        name="table",
    )(work)


def reverse(i, bits):
    return int(format(i, f"0{bits}b")[::-1], 2) if bits else 0


def spread(pieces, level):
    distance = 1 << level
    if len(pieces) <= 4:
        arrived = []
        for piece in pieces:
            arrived.append(swapped(piece, "row", distance))
        return pieces + arrived
    arrived = swapped(jnp.stack(pieces), "row", distance)
    return pieces + [arrived[i] for i in range(len(pieces))]


def body(panel, signs, offsets, owners):
    width, row_count = panel.shape
    devices = lax.axis_size("row")
    bits = devices.bit_length() - 1
    count = offsets.shape[0]
    group = LANES // width
    per = count // group
    near = min(bits, 2)
    listed = [offsets]
    for t in range(1, 1 << near):
        listed.append(swapped(offsets, "row", t))
    work = transform_rows(panel, signs)
    for level in range(near, bits):
        listed = spread(listed, level)
    table = transform_table(work, width)

    def pick(slots):
        return pl.pallas_call(
            functools.partial(pick_kernel, width, slots, count, len(slots) <= 4),
            out_shape=jax.ShapeDtypeStruct((len(slots) * per, LANES), f32),
            in_specs=[SMEM] * len(slots) + [VMEM],
            out_specs=VMEM,
            compiler_params=PARAMS,
            name="pick",
        )(*[listed[t] for t in slots], table)

    chunks = []
    for upper in range(2):
        odd = list(range(1 + upper * devices // 2, (1 + upper) * devices // 2, 2))
        odd.sort(key=lambda t: reverse(t, bits))
        chunks.append((odd, swapped(pick(odd), "row", 1)))
    kept = [pick([t - 1 for t in odd]) for odd, _ in chunks]
    totals = []
    for mine, (_, arrived) in zip(kept, chunks):
        total = mine + arrived
        for level in range(1, bits - 1):
            middle = total.shape[0] // 2
            total = total[:middle] + swapped(total[middle:], "row", 1 << level)
        totals.append(total)
    total = totals[0] + swapped(totals[1], "row", devices // 2)
    col_bits = lax.axis_size("col").bit_length() - 1
    stacked = total[None]
    for level in reversed(range(col_bits)):
        stacked = jnp.concatenate([stacked, swapped(stacked, "col", 1 << level)], axis=0)
    packed = [stacked[reverse(u, col_bits)] for u in range(group)]
    scale = 1.0 / (devices * row_count * count)
    gram = pl.pallas_call(
        functools.partial(gram_kernel, width, count, devices, scale),
        out_shape=jax.ShapeDtypeStruct((devices * width, LANES), f32),
        in_specs=[VMEM] * (1 + group),
        out_specs=VMEM,
        compiler_params=PARAMS,
        name="gram",
    )(owners, *packed)
    gram = gram.reshape(1 << near, devices >> near, width, LANES)
    total = gram[0]
    for t in range(1, 1 << near):
        total = total + swapped(gram[t], "row", t)
    for level in reversed(range(near, bits)):
        middle = total.shape[0] // 2
        total = total[:middle] + swapped(total[middle:], "row", 1 << level)
    return total


def solution(mesh):
    placed = (P("col", "row"), P("row"), P("row"), P("row", None))
    return jax.shard_map(
        body, mesh=mesh, in_specs=placed, out_specs=P("row", "col", None), check_vma=False
    )
```

```python
import functools

import jax
import jax.numpy as jnp
from jax import lax
from jax.experimental import pallas as pl
from jax.experimental.pallas import tpu as pltpu
from jax.sharding import PartitionSpec as P


LANES = 128
f32, bf16 = jnp.float32, jnp.bfloat16


def swapped(x, axis, distance):
    return lax.ppermute(x, axis, [(i, i ^ distance) for i in range(lax.axis_size(axis))])


def parity(v):
    v = v ^ (v >> 8)
    v = v ^ (v >> 4)
    v = v ^ (v >> 2)
    v = v ^ (v >> 1)
    return v & 1


def butterflies(values):
    step = 1
    while step < len(values):
        out = list(values)
        for i in range(len(values)):
            if not i & step:
                out[i] = values[i] + values[i | step]
                out[i | step] = values[i] - values[i | step]
        values = out
        step *= 2
    return values


def halves(x):
    top = x.astype(bf16)
    return top, (x - top.astype(f32)).astype(bf16)


def rows_kernel(width, x_ref, sign_ref, work_ref):
    def some(lo, _):
        signs = [sign_ref[pl.ds(hi * 8 + lo, 1), :].astype(f32) for hi in range(16)]
        for band in range(width // 8):
            rows = pl.ds(band * 8, 8)
            values = []
            for hi in range(16):
                start = pl.multiple_of((hi * 8 + lo) * LANES, LANES)
                values.append(x_ref[rows, pl.ds(start, LANES)] * signs[hi])
            for hi, value in enumerate(butterflies(values)):
                work_ref[hi * 8 + lo, rows, :] = value
        return 0

    lax.fori_loop(0, 8, some, 0)


def table_kernel(width, work_ref, table_ref):
    group = LANES // width
    bands = width // 8
    row = lax.broadcasted_iota(jnp.int32, (LANES, 2 * LANES), 0)
    column = lax.broadcasted_iota(jnp.int32, (LANES, 2 * LANES), 1)
    hadamard = (1 - 2 * parity(row & (column & (LANES - 1)))).astype(f32).astype(bf16)
    lane = lax.broadcasted_iota(jnp.int32, (LANES, LANES), 1) // width
    in_lane = [lane == g for g in range(group)]
    repeating = 4 if width * 8 > LANES else 8

    def times(top, low):
        both = jnp.concatenate([top, low], axis=1)
        return lax.dot_general(hadamard, both, (((1,), (1,)), ((), ())), preferred_element_type=f32)

    def some(hi, _):
        rows = [
            butterflies([work_ref[hi * 8 + lo, pl.ds(band * 8, 8), :] for lo in range(8)]) for band in range(bands)
        ]
        y = jnp.concatenate([rows[band][lo] for lo in range(8) for band in range(bands)], axis=0)
        top, low = halves(y)
        results = []
        for e in range(0, repeating, 2):
            parts = [
                jnp.concatenate([v[(e + i) * width : (e + i + 1) * width] for i in range(2) for _ in range(group)])
                for v in (top, low)
            ]
            mixed = times(*parts)
            results += [mixed[:, :LANES], mixed[:, LANES:]]
        for e in range(repeating, 8, group):
            mixed = times(top[e * width :][:LANES], low[e * width :][:LANES])
            turned = [mixed] + [pltpu.roll(mixed, k * width, 1) for k in range(1, group)]
            for i in range(group):
                total = turned[-i % group]
                for g in range(1, group):
                    total = jnp.where(in_lane[g], turned[(g - i) % group], total)
                results.append(total)
        for e, result in enumerate(results):
            table_ref[pl.ds(pl.multiple_of((hi * 8 + e) * LANES, LANES), LANES), :] = result
        return 0

    lax.fori_loop(0, 16, some, 0, unroll=4)


def pick_kernel(width, slots, count, straight, *refs):
    offset_refs, table_ref, out_ref = refs[:-2], refs[-2], refs[-1]
    group = LANES // width
    per = count // group
    lane = lax.broadcasted_iota(jnp.int32, (8, LANES), 1) // width
    sub = lax.broadcasted_iota(jnp.int32, (8, LANES), 0)
    in_sub = [sub == s for s in range(8)]
    in_lane = [lane == g for g in range(group)]
    me = lax.axis_index("row")
    for place, slot in enumerate(slots):
        sign = (1 - 2 * parity(me & (me ^ slot))).astype(f32)

        def block(inner):
            total = None
            for g in range(group):
                part = None
                for s in range(8):
                    spot = offset_refs[place][inner + (g * per + s)]
                    value = jnp.broadcast_to(table_ref[pl.ds(spot, 1), :], (8, LANES))
                    part = value if part is None else jnp.where(in_sub[s], value, part)
                total = part if total is None else jnp.where(in_lane[g], part, total)
            return total * sign

        if straight:
            for inner in range(0, per, 8):
                out_ref[pl.ds(place * per + inner, 8), :] = block(inner)
        else:

            def some(it, _):
                inner = pl.multiple_of(it * 8, 8)
                out_ref[pl.ds(place * per + inner, 8), :] = block(inner)
                return 0

            lax.fori_loop(0, per // 8, some, 0)


def gram_kernel(width, count, named, scale, owner_ref, *refs):
    group = LANES // width
    per = count // group
    packed, out_ref = refs[:-1], refs[-1]
    lane = lax.broadcasted_iota(jnp.int32, (per, LANES), 1)
    parts, repeated = [], []
    for g in range(group):
        total = packed[g][...]
        for u in range(group):
            if u != g:
                moved = jnp.take_along_axis(packed[u][...], lane ^ ((u ^ g) * width), axis=1)
                total = jnp.where(lane // width == u, moved, total)
        parts.append(total)
        repeated.append(jnp.take_along_axis(packed[0][...], (lane & (width - 1)) + g * width, axis=1))
    sketch = jnp.concatenate(parts, axis=0)
    mine = jnp.concatenate(repeated, axis=0)
    top, low = halves(sketch)
    mine_top, mine_low = halves(mine)
    whose = jnp.broadcast_to(owner_ref[...], (count, LANES))
    tall = lax.broadcasted_iota(jnp.int32, (count, LANES), 1) // width
    zero = jnp.zeros((count, LANES), bf16)
    me, col = lax.axis_index("row"), lax.axis_index("col")
    turned = lax.broadcasted_iota(jnp.int32, (LANES, LANES), 1) ^ (col * width)
    over = (((0,), (0,)), ((), ()))
    for block in range(named * width // LANES):
        match = whose == tall + block * group
        left = jnp.where(match, mine_top, zero)
        gram = lax.dot_general(left, top, over, preferred_element_type=f32)
        gram = gram + lax.dot_general(left, low, over, preferred_element_type=f32)
        left = jnp.where(match, mine_low, zero)
        gram = gram + lax.dot_general(left, top, over, preferred_element_type=f32)
        gram = jnp.take_along_axis(gram, turned, axis=1) * scale
        for k in range(group):
            slot = (block * group + k) ^ me
            place = (slot & 3) * (named // 4) + (slot >> 2)
            out_ref[pl.ds(pl.multiple_of(place * width, 8), width), :] = gram[k * width : (k + 1) * width]


VMEM = pl.BlockSpec(memory_space=pltpu.VMEM)
SMEM = pl.BlockSpec(memory_space=pltpu.SMEM)
PARAMS = pltpu.CompilerParams(vmem_limit_bytes=24 << 20)


def transform_rows(panel, signs):
    width, _ = panel.shape
    return pl.pallas_call(
        functools.partial(rows_kernel, width),
        out_shape=jax.ShapeDtypeStruct((LANES, width, LANES), f32),
        in_specs=[VMEM] * 2,
        out_specs=VMEM,
        compiler_params=PARAMS,
        name="rows",
    )(panel, signs.reshape(LANES, LANES))


def transform_table(work, width):
    return pl.pallas_call(
        functools.partial(table_kernel, width),
        out_shape=jax.ShapeDtypeStruct((LANES * LANES, LANES), f32),
        in_specs=[VMEM],
        out_specs=VMEM,
        compiler_params=PARAMS,
        name="table",
    )(work)


def reverse(i, bits):
    return int(format(i, f"0{bits}b")[::-1], 2) if bits else 0


def spread(pieces, level):
    distance = 1 << level
    if len(pieces) <= 4:
        arrived = []
        for piece in pieces:
            arrived.append(swapped(piece, "row", distance))
        return pieces + arrived
    arrived = swapped(jnp.stack(pieces), "row", distance)
    return pieces + [arrived[i] for i in range(len(pieces))]


def body(panel, signs, offsets, owners):
    width, row_count = panel.shape
    devices = lax.axis_size("row")
    bits = devices.bit_length() - 1
    count = offsets.shape[0]
    group = LANES // width
    per = count // group
    near = min(bits, 2)
    listed = [offsets]
    for t in range(1, 1 << near):
        listed.append(swapped(offsets, "row", t))
    work = transform_rows(panel, signs)
    for level in range(near, bits):
        listed = spread(listed, level)
    table = transform_table(work, width)

    def pick(slots):
        return pl.pallas_call(
            functools.partial(pick_kernel, width, slots, count, len(slots) <= 4),
            out_shape=jax.ShapeDtypeStruct((len(slots) * per, LANES), f32),
            in_specs=[SMEM] * len(slots) + [VMEM],
            out_specs=VMEM,
            compiler_params=PARAMS,
            name="pick",
        )(*[listed[t] for t in slots], table)

    chunks = []
    for upper in range(2):
        odd = list(range(1 + upper * devices // 2, (1 + upper) * devices // 2, 2))
        odd.sort(key=lambda t: reverse(t, bits))
        chunks.append((odd, swapped(pick(odd), "row", 1)))
    kept = [pick([t - 1 for t in odd]) for odd, _ in chunks]
    totals = []
    for mine, (_, arrived) in zip(kept, chunks):
        total = mine + arrived
        for level in range(1, bits - 1):
            middle = total.shape[0] // 2
            total = total[:middle] + swapped(total[middle:], "row", 1 << level)
        totals.append(total)
    total = totals[0] + swapped(totals[1], "row", devices // 2)
    col_bits = lax.axis_size("col").bit_length() - 1
    stacked = total[None]
    for level in reversed(range(col_bits)):
        stacked = jnp.concatenate([stacked, swapped(stacked, "col", 1 << level)], axis=0)
    packed = [stacked[reverse(u, col_bits)] for u in range(group)]
    scale = 1.0 / (devices * row_count * count)
    gram = pl.pallas_call(
        functools.partial(gram_kernel, width, count, devices, scale),
        out_shape=jax.ShapeDtypeStruct((devices * width, LANES), f32),
        in_specs=[VMEM] * (1 + group),
        out_specs=VMEM,
        compiler_params=PARAMS,
        name="gram",
    )(owners, *packed)
    gram = gram.reshape(1 << near, devices >> near, width, LANES)
    total = gram[0]
    for t in range(1, 1 << near):
        total = total + swapped(gram[t], "row", t)
    for level in reversed(range(near, bits)):
        middle = total.shape[0] // 2
        total = total[:middle] + swapped(total[middle:], "row", 1 << level)
    return total


def solution(mesh):
    placed = (P("col", "row"), P("row"), P("row"), P("row", None))
    return jax.shard_map(
        body, mesh=mesh, in_specs=placed, out_specs=P("row", "col", None), check_vma=False
    )
```

```python
import functools

import jax
import jax.numpy as jnp
from jax import lax
from jax.experimental import pallas as pl
from jax.experimental.pallas import tpu as pltpu
from jax.sharding import PartitionSpec as P


LANES = 128
f32, bf16 = jnp.float32, jnp.bfloat16


def swapped(x, axis, distance):
    return lax.ppermute(x, axis, [(i, i ^ distance) for i in range(lax.axis_size(axis))])


def parity(v):
    v = v ^ (v >> 8)
    v = v ^ (v >> 4)
    v = v ^ (v >> 2)
    v = v ^ (v >> 1)
    return v & 1


def butterflies(values):
    step = 1
    while step < len(values):
        out = list(values)
        for i in range(len(values)):
            if not i & step:
                out[i] = values[i] + values[i | step]
                out[i | step] = values[i] - values[i | step]
        values = out
        step *= 2
    return values


def halves(x):
    top = x.astype(bf16)
    return top, (x - top.astype(f32)).astype(bf16)


def rows_kernel(width, x_ref, sign_ref, work_ref):
    def some(lo, _):
        signs = [sign_ref[pl.ds(hi * 8 + lo, 1), :].astype(f32) for hi in range(16)]
        for band in range(width // 8):
            rows = pl.ds(band * 8, 8)
            values = []
            for hi in range(16):
                start = pl.multiple_of((hi * 8 + lo) * LANES, LANES)
                values.append(x_ref[rows, pl.ds(start, LANES)] * signs[hi])
            for hi, value in enumerate(butterflies(values)):
                work_ref[hi * 8 + lo, rows, :] = value
        return 0

    lax.fori_loop(0, 8, some, 0)


def table_kernel(width, work_ref, table_ref):
    group = LANES // width
    bands = width // 8
    row = lax.broadcasted_iota(jnp.int32, (LANES, 2 * LANES), 0)
    column = lax.broadcasted_iota(jnp.int32, (LANES, 2 * LANES), 1)
    hadamard = (1 - 2 * parity(row & (column & (LANES - 1)))).astype(f32).astype(bf16)
    lane = lax.broadcasted_iota(jnp.int32, (LANES, LANES), 1) // width
    in_lane = [lane == g for g in range(group)]
    repeating = 4 if width * 8 > LANES else 8

    def times(top, low):
        both = jnp.concatenate([top, low], axis=1)
        return lax.dot_general(hadamard, both, (((1,), (1,)), ((), ())), preferred_element_type=f32)

    def some(hi, _):
        rows = [
            butterflies([work_ref[hi * 8 + lo, pl.ds(band * 8, 8), :] for lo in range(8)]) for band in range(bands)
        ]
        y = jnp.concatenate([rows[band][lo] for lo in range(8) for band in range(bands)], axis=0)
        top, low = halves(y)
        results = []
        for e in range(0, repeating, 2):
            parts = [
                jnp.concatenate([v[(e + i) * width : (e + i + 1) * width] for i in range(2) for _ in range(group)])
                for v in (top, low)
            ]
            mixed = times(*parts)
            results += [mixed[:, :LANES], mixed[:, LANES:]]
        for e in range(repeating, 8, group):
            mixed = times(top[e * width :][:LANES], low[e * width :][:LANES])
            turned = [mixed] + [pltpu.roll(mixed, k * width, 1) for k in range(1, group)]
            for i in range(group):
                total = turned[-i % group]
                for g in range(1, group):
                    total = jnp.where(in_lane[g], turned[(g - i) % group], total)
                results.append(total)
        for e, result in enumerate(results):
            table_ref[pl.ds(pl.multiple_of((hi * 8 + e) * LANES, LANES), LANES), :] = result
        return 0

    lax.fori_loop(0, 16, some, 0, unroll=4)


def pick_kernel(width, slots, spots, count, first, rows, straight, *refs):
    offset_refs, table_ref, out_ref = refs[:-2], refs[-2], refs[-1]
    group = LANES // width
    per = count // group
    lane = lax.broadcasted_iota(jnp.int32, (8, LANES), 1) // width
    sub = lax.broadcasted_iota(jnp.int32, (8, LANES), 0)
    in_sub = [sub == s for s in range(8)]
    in_lane = [lane == g for g in range(group)]
    me = lax.axis_index("row")
    for place, slot in enumerate(slots):
        sign = (1 - 2 * parity(me & (me ^ slot))).astype(f32)
        which, base = spots[place]

        def block(inner):
            total = None
            for g in range(group):
                part = None
                for s in range(8):
                    spot = offset_refs[which][inner + (base + first + g * per + s)]
                    value = jnp.broadcast_to(table_ref[pl.ds(spot, 1), :], (8, LANES))
                    part = value if part is None else jnp.where(in_sub[s], value, part)
                total = part if total is None else jnp.where(in_lane[g], part, total)
            return total * sign

        if straight:
            for inner in range(0, rows, 8):
                out_ref[pl.ds(place * rows + inner, 8), :] = block(inner)
        else:

            def some(it, _):
                inner = pl.multiple_of(it * 8, 8)
                out_ref[pl.ds(place * rows + inner, 8), :] = block(inner)
                return 0

            lax.fori_loop(0, rows // 8, some, 0)


def gram_kernel(width, count, named, scale, owner_ref, *refs):
    group = LANES // width
    per = count // group
    packed, out_ref = refs[:-1], refs[-1]
    lane = lax.broadcasted_iota(jnp.int32, (per, LANES), 1)
    parts, repeated = [], []
    for g in range(group):
        total = packed[g][...]
        for u in range(group):
            if u != g:
                moved = jnp.take_along_axis(packed[u][...], lane ^ ((u ^ g) * width), axis=1)
                total = jnp.where(lane // width == u, moved, total)
        parts.append(total)
        repeated.append(jnp.take_along_axis(packed[0][...], (lane & (width - 1)) + g * width, axis=1))
    sketch = jnp.concatenate(parts, axis=0)
    mine = jnp.concatenate(repeated, axis=0)
    top, low = halves(sketch)
    mine_top, mine_low = halves(mine)
    whose = jnp.broadcast_to(owner_ref[...], (count, LANES))
    tall = lax.broadcasted_iota(jnp.int32, (count, LANES), 1) // width
    zero = jnp.zeros((count, LANES), bf16)
    me, col = lax.axis_index("row"), lax.axis_index("col")
    turned = lax.broadcasted_iota(jnp.int32, (LANES, LANES), 1) ^ (col * width)
    over = (((0,), (0,)), ((), ()))
    for block in range(named * width // LANES):
        match = whose == tall + block * group
        left = jnp.where(match, mine_top, zero)
        gram = lax.dot_general(left, top, over, preferred_element_type=f32)
        gram = gram + lax.dot_general(left, low, over, preferred_element_type=f32)
        left = jnp.where(match, mine_low, zero)
        gram = gram + lax.dot_general(left, top, over, preferred_element_type=f32)
        gram = jnp.take_along_axis(gram, turned, axis=1) * scale
        for k in range(group):
            slot = (block * group + k) ^ me
            place = (slot & 3) * (named // 4) + (slot >> 2)
            out_ref[pl.ds(pl.multiple_of(place * width, 8), width), :] = gram[k * width : (k + 1) * width]


VMEM = pl.BlockSpec(memory_space=pltpu.VMEM)
SMEM = pl.BlockSpec(memory_space=pltpu.SMEM)
PARAMS = pltpu.CompilerParams(vmem_limit_bytes=24 << 20)


def transform_rows(panel, signs):
    width, _ = panel.shape
    return pl.pallas_call(
        functools.partial(rows_kernel, width),
        out_shape=jax.ShapeDtypeStruct((LANES, width, LANES), f32),
        in_specs=[VMEM] * 2,
        out_specs=VMEM,
        compiler_params=PARAMS,
        name="rows",
    )(panel, signs.reshape(LANES, LANES))


def transform_table(work, width):
    return pl.pallas_call(
        functools.partial(table_kernel, width),
        out_shape=jax.ShapeDtypeStruct((LANES * LANES, LANES), f32),
        in_specs=[VMEM],
        out_specs=VMEM,
        compiler_params=PARAMS,
        name="table",
    )(work)


def reverse(i, bits):
    return int(format(i, f"0{bits}b")[::-1], 2) if bits else 0


def body(panel, signs, offsets, owners):
    width, row_count = panel.shape
    devices = lax.axis_size("row")
    bits = devices.bit_length() - 1
    count = offsets.shape[0]
    group = LANES // width
    per = count // group
    near = min(bits, 2)
    listed = [offsets]
    for t in range(1, 1 << near):
        listed.append(swapped(offsets, "row", t))
    work = transform_rows(panel, signs)
    arrays, entries = list(listed), [(t, 0) for t in range(1 << near)]
    if bits > near:
        far = jnp.concatenate(listed)
        far = swapped(far, "row", 1 << near)
        arrays.append(far)
        entries += [(len(arrays) - 1, t * count) for t in range(1 << near)]
        for level in range(near + 1, bits):
            held = jnp.concatenate([arrays[k][at : at + count] for k, at in entries])
            arrays.append(swapped(held, "row", 1 << level))
            entries += [(len(arrays) - 1, t * count) for t in range(1 << level)]
    table = transform_table(work, width)

    def pick(slots, first, rows):
        used = sorted({entries[t][0] for t in slots})
        spots = [(used.index(entries[t][0]), entries[t][1]) for t in slots]
        straight = len(slots) * rows * group <= 4096
        return pl.pallas_call(
            functools.partial(pick_kernel, width, slots, spots, count, first, rows, straight),
            out_shape=jax.ShapeDtypeStruct((len(slots) * rows, LANES), f32),
            in_specs=[SMEM] * len(used) + [VMEM],
            out_specs=VMEM,
            compiler_params=PARAMS,
            name="pick",
        )(*[arrays[k] for k in used], table)

    order = sorted(range(1, devices, 2), key=lambda t: reverse(t, bits))
    upper = [t for t in order if t >= devices // 2]
    lower = [t for t in order if t < devices // 2]
    chunks = [(upper, 0, per // 2), (upper, per // 2, per // 2), (lower, 0, per)]
    arrived = []
    for chunk in chunks:
        sent = pick(*chunk)
        arrived.append(swapped(sent, "row", 1))
    totals = []
    for (odd, first, rows), other in zip(chunks, arrived):
        total = pick([t - 1 for t in odd], first, rows) + other
        for level in range(1, bits - 1):
            middle = total.shape[0] // 2
            other = swapped(total[middle:], "row", 1 << level)
            total = total[:middle] + other
        totals.append(total)
    col_size = lax.axis_size("col")
    col_bits = col_size.bit_length() - 1
    own, other = [], []
    for part in range(2):
        mine = totals[2][part * per // 2 : (part + 1) * per // 2]
        if part:
            mine, own[0] = lax.optimization_barrier((mine, own[0]))
        own.append(mine + swapped(totals[part], "row", devices // 2))
        other.append(swapped(own[part], "col", col_size // 2))
    stacked = jnp.stack([jnp.concatenate(own), jnp.concatenate(other)])
    for level in reversed(range(col_bits - 1)):
        stacked = jnp.concatenate([stacked, swapped(stacked, "col", 1 << level)], axis=0)
    packed = [stacked[reverse(u, col_bits)] for u in range(group)]
    scale = 1.0 / (devices * row_count * count)
    gram = pl.pallas_call(
        functools.partial(gram_kernel, width, count, devices, scale),
        out_shape=jax.ShapeDtypeStruct((devices * width, LANES), f32),
        in_specs=[VMEM] * (1 + group),
        out_specs=VMEM,
        compiler_params=PARAMS,
        name="gram",
    )(owners, *packed)
    gram = gram.reshape(1 << near, devices >> near, width, LANES)
    total = gram[0]
    for t in range(1, 1 << near):
        total = total + swapped(gram[t], "row", t)
    for level in reversed(range(near, bits)):
        middle = total.shape[0] // 2
        total = total[:middle] + swapped(total[middle:], "row", 1 << level)
    return total


def solution(mesh):
    placed = (P("col", "row"), P("row"), P("row"), P("row", None))
    return jax.shard_map(
        body, mesh=mesh, in_specs=placed, out_specs=P("row", "col", None), check_vma=False
    )
```

```python
import functools

import jax
import jax.numpy as jnp
from jax import lax
from jax.experimental import pallas as pl
from jax.experimental.pallas import tpu as pltpu
from jax.sharding import PartitionSpec as P


LANES = 128
f32, bf16 = jnp.float32, jnp.bfloat16


def swapped(x, axis, distance):
    return lax.ppermute(x, axis, [(i, i ^ distance) for i in range(lax.axis_size(axis))])


def parity(v):
    v = v ^ (v >> 8)
    v = v ^ (v >> 4)
    v = v ^ (v >> 2)
    v = v ^ (v >> 1)
    return v & 1


def butterflies(values):
    step = 1
    while step < len(values):
        out = list(values)
        for i in range(len(values)):
            if not i & step:
                out[i] = values[i] + values[i | step]
                out[i | step] = values[i] - values[i | step]
        values = out
        step *= 2
    return values


def halves(x):
    top = x.astype(bf16)
    return top, (x - top.astype(f32)).astype(bf16)


def rows_kernel(width, x_ref, sign_ref, work_ref):
    def some(lo, _):
        signs = [sign_ref[pl.ds(hi * 8 + lo, 1), :].astype(f32) for hi in range(16)]
        for band in range(width // 8):
            rows = pl.ds(band * 8, 8)
            values = []
            for hi in range(16):
                start = pl.multiple_of((hi * 8 + lo) * LANES, LANES)
                values.append(x_ref[rows, pl.ds(start, LANES)] * signs[hi])
            for hi, value in enumerate(butterflies(values)):
                work_ref[hi * 8 + lo, rows, :] = value
        return 0

    lax.fori_loop(0, 8, some, 0)


def table_kernel(width, work_ref, table_ref):
    group = LANES // width
    bands = width // 8
    row = lax.broadcasted_iota(jnp.int32, (LANES, 2 * LANES), 0)
    column = lax.broadcasted_iota(jnp.int32, (LANES, 2 * LANES), 1)
    hadamard = (1 - 2 * parity(row & (column & (LANES - 1)))).astype(f32).astype(bf16)
    lane = lax.broadcasted_iota(jnp.int32, (LANES, LANES), 1) // width
    in_lane = [lane == g for g in range(group)]
    repeating = 4 if width * 8 > LANES else 8

    def times(top, low):
        both = jnp.concatenate([top, low], axis=1)
        return lax.dot_general(hadamard, both, (((1,), (1,)), ((), ())), preferred_element_type=f32)

    def some(hi, _):
        rows = [
            butterflies([work_ref[hi * 8 + lo, pl.ds(band * 8, 8), :] for lo in range(8)]) for band in range(bands)
        ]
        y = jnp.concatenate([rows[band][lo] for lo in range(8) for band in range(bands)], axis=0)
        top, low = halves(y)
        results = []
        for e in range(0, repeating, 2):
            parts = [
                jnp.concatenate([v[(e + i) * width : (e + i + 1) * width] for i in range(2) for _ in range(group)])
                for v in (top, low)
            ]
            mixed = times(*parts)
            results += [mixed[:, :LANES], mixed[:, LANES:]]
        for e in range(repeating, 8, group):
            mixed = times(top[e * width :][:LANES], low[e * width :][:LANES])
            turned = [mixed] + [pltpu.roll(mixed, k * width, 1) for k in range(1, group)]
            for i in range(group):
                total = turned[-i % group]
                for g in range(1, group):
                    total = jnp.where(in_lane[g], turned[(g - i) % group], total)
                results.append(total)
        for e, result in enumerate(results):
            table_ref[pl.ds(pl.multiple_of((hi * 8 + e) * LANES, LANES), LANES), :] = result
        return 0

    lax.fori_loop(0, 16, some, 0, unroll=4)


def pick_kernel(width, pieces, count, straight, *refs):
    offset_refs, table_ref, out_refs = refs[: -1 - len(pieces)], refs[-1 - len(pieces)], refs[-len(pieces) :]
    group = LANES // width
    per = count // group
    lane = lax.broadcasted_iota(jnp.int32, (8, LANES), 1) // width
    sub = lax.broadcasted_iota(jnp.int32, (8, LANES), 0)
    in_sub = [sub == s for s in range(8)]
    in_lane = [lane == g for g in range(group)]
    me = lax.axis_index("row")
    for out_ref, (slots, first, rows) in zip(out_refs, pieces):
        for place, (slot, which, base) in enumerate(slots):
            sign = (1 - 2 * parity(me & (me ^ slot))).astype(f32)

            def block(inner):
                total = None
                for g in range(group):
                    part = None
                    for s in range(8):
                        spot = offset_refs[which][inner + (base + first + g * per + s)]
                        value = jnp.broadcast_to(table_ref[pl.ds(spot, 1), :], (8, LANES))
                        part = value if part is None else jnp.where(in_sub[s], value, part)
                    total = part if total is None else jnp.where(in_lane[g], part, total)
                return total * sign

            if straight:
                for inner in range(0, rows, 8):
                    out_ref[pl.ds(place * rows + inner, 8), :] = block(inner)
            else:

                def some(it, _):
                    inner = pl.multiple_of(it * 8, 8)
                    out_ref[pl.ds(place * rows + inner, 8), :] = block(inner)
                    return 0

                lax.fori_loop(0, rows // 8, some, 0)


def gram_kernel(width, count, named, scale, owner_ref, *refs):
    group = LANES // width
    per = count // group
    packed, out_ref = refs[:-1], refs[-1]
    lane = lax.broadcasted_iota(jnp.int32, (per, LANES), 1)
    parts, repeated = [], []
    for g in range(group):
        total = packed[g][...]
        for u in range(group):
            if u != g:
                moved = jnp.take_along_axis(packed[u][...], lane ^ ((u ^ g) * width), axis=1)
                total = jnp.where(lane // width == u, moved, total)
        parts.append(total)
        repeated.append(jnp.take_along_axis(packed[0][...], (lane & (width - 1)) + g * width, axis=1))
    sketch = jnp.concatenate(parts, axis=0)
    mine = jnp.concatenate(repeated, axis=0)
    top, low = halves(sketch)
    mine_top, mine_low = halves(mine)
    whose = jnp.broadcast_to(owner_ref[...], (count, LANES))
    tall = lax.broadcasted_iota(jnp.int32, (count, LANES), 1) // width
    zero = jnp.zeros((count, LANES), bf16)
    me, col = lax.axis_index("row"), lax.axis_index("col")
    turned = lax.broadcasted_iota(jnp.int32, (LANES, LANES), 1) ^ (col * width)
    over = (((0,), (0,)), ((), ()))
    for block in range(named * width // LANES):
        match = whose == tall + block * group
        left = jnp.where(match, mine_top, zero)
        gram = lax.dot_general(left, top, over, preferred_element_type=f32)
        gram = gram + lax.dot_general(left, low, over, preferred_element_type=f32)
        left = jnp.where(match, mine_low, zero)
        gram = gram + lax.dot_general(left, top, over, preferred_element_type=f32)
        gram = jnp.take_along_axis(gram, turned, axis=1) * scale
        for k in range(group):
            slot = (block * group + k) ^ me
            place = (slot & 3) * (named // 4) + (slot >> 2)
            out_ref[pl.ds(pl.multiple_of(place * width, 8), width), :] = gram[k * width : (k + 1) * width]


VMEM = pl.BlockSpec(memory_space=pltpu.VMEM)
SMEM = pl.BlockSpec(memory_space=pltpu.SMEM)
PARAMS = pltpu.CompilerParams(vmem_limit_bytes=24 << 20)


def transform_rows(panel, signs):
    width, _ = panel.shape
    return pl.pallas_call(
        functools.partial(rows_kernel, width),
        out_shape=jax.ShapeDtypeStruct((LANES, width, LANES), f32),
        in_specs=[VMEM] * 2,
        out_specs=VMEM,
        compiler_params=PARAMS,
        name="rows",
    )(panel, signs.reshape(LANES, LANES))


def transform_table(work, width):
    return pl.pallas_call(
        functools.partial(table_kernel, width),
        out_shape=jax.ShapeDtypeStruct((LANES * LANES, LANES), f32),
        in_specs=[VMEM],
        out_specs=VMEM,
        compiler_params=PARAMS,
        name="table",
    )(work)


def reverse(i, bits):
    return int(format(i, f"0{bits}b")[::-1], 2) if bits else 0


def body(panel, signs, offsets, owners):
    width, row_count = panel.shape
    devices = lax.axis_size("row")
    bits = devices.bit_length() - 1
    count = offsets.shape[0]
    group = LANES // width
    per = count // group
    near = min(bits, 2)
    listed = [offsets]
    for t in range(1, 1 << near):
        listed.append(swapped(offsets, "row", t))
    work = transform_rows(panel, signs)
    arrays, entries = list(listed), [(t, 0) for t in range(1 << near)]
    if bits > near:
        far = jnp.concatenate(listed)
        far = swapped(far, "row", 1 << near)
        arrays.append(far)
        entries += [(len(arrays) - 1, t * count) for t in range(1 << near)]
        for level in range(near + 1, bits):
            held = jnp.concatenate([arrays[k][at : at + count] for k, at in entries])
            arrays.append(swapped(held, "row", 1 << level))
            entries += [(len(arrays) - 1, t * count) for t in range(1 << level)]
    table = transform_table(work, width)

    def pick(*pieces):
        used = sorted({entries[t][0] for slots, _, _ in pieces for t in slots})
        full = [
            ([(t, used.index(entries[t][0]), entries[t][1]) for t in slots], first, rows)
            for slots, first, rows in pieces
        ]
        straight = sum(len(slots) * rows for slots, _, rows in pieces) * group <= 4096
        return pl.pallas_call(
            functools.partial(pick_kernel, width, full, count, straight),
            out_shape=[jax.ShapeDtypeStruct((len(slots) * rows, LANES), f32) for slots, _, rows in pieces],
            in_specs=[SMEM] * len(used) + [VMEM],
            out_specs=[VMEM] * len(pieces),
            compiler_params=PARAMS,
            name="pick",
        )(*[arrays[k] for k in used], table)

    def split(slots, levels):
        slots = sorted(slots, key=lambda t: [t >> level & 1 for level in levels])
        return slots[: len(slots) // 2], slots[len(slots) // 2 :]

    levels = list(range(bits - 1))
    turned = [1, 0] + levels[2:] if bits > 2 else levels
    half = per // 2
    keep_up, send_up = split(range(devices // 2, devices), levels)
    keep_low, send_low = split(range(devices // 2), turned)
    sent, kept = [None] * 3, [None] * 3
    sent[0], kept[0] = pick((send_up, 0, half), (keep_up, 0, half))
    sent[1], sent[2], kept[1] = pick((send_up, half, half), (send_low, 0, per), (keep_up, half, half))
    (kept[2],) = pick((keep_low, 0, per))
    totals = []
    for k, order in enumerate((levels, levels, turned)):
        total, out = kept[k], sent[k]
        for step, level in enumerate(order):
            if step:
                middle = total.shape[0] // 2
                total, out = total[:middle], total[middle:]
            other = swapped(out, "row", 1 << level)
            total = total + other
        totals.append(total)
    col_size = lax.axis_size("col")
    col_bits = col_size.bit_length() - 1
    own, other = [], []
    for part in range(2):
        mine = totals[2][part * per // 2 : (part + 1) * per // 2]
        if part:
            mine, own[0] = lax.optimization_barrier((mine, own[0]))
        own.append(mine + swapped(totals[part], "row", devices // 2))
        other.append(swapped(own[part], "col", col_size // 2))
    stacked = jnp.stack([jnp.concatenate(own), jnp.concatenate(other)])
    for level in reversed(range(col_bits - 1)):
        stacked = jnp.concatenate([stacked, swapped(stacked, "col", 1 << level)], axis=0)
    packed = [stacked[reverse(u, col_bits)] for u in range(group)]
    scale = 1.0 / (devices * row_count * count)
    gram = pl.pallas_call(
        functools.partial(gram_kernel, width, count, devices, scale),
        out_shape=jax.ShapeDtypeStruct((devices * width, LANES), f32),
        in_specs=[VMEM] * (1 + group),
        out_specs=VMEM,
        compiler_params=PARAMS,
        name="gram",
    )(owners, *packed)
    gram = gram.reshape(1 << near, devices >> near, width, LANES)
    total = gram[0]
    for t in range(1, 1 << near):
        total = total + swapped(gram[t], "row", t)
    for level in reversed(range(near, bits)):
        middle = total.shape[0] // 2
        total = total[:middle] + swapped(total[middle:], "row", 1 << level)
    return total


def solution(mesh):
    placed = (P("col", "row"), P("row"), P("row"), P("row", None))
    return jax.shard_map(body, mesh=mesh, in_specs=placed, out_specs=P("row", "col", None), check_vma=False)
```

```python
import functools

import jax
import jax.numpy as jnp
from jax import lax
from jax.experimental import pallas as pl
from jax.experimental.pallas import tpu as pltpu
from jax.sharding import PartitionSpec as P


LANES = 128
f32, bf16 = jnp.float32, jnp.bfloat16


def swapped(x, axis, distance):
    return lax.ppermute(x, axis, [(i, i ^ distance) for i in range(lax.axis_size(axis))])


def parity(v):
    v = v ^ (v >> 8)
    v = v ^ (v >> 4)
    v = v ^ (v >> 2)
    v = v ^ (v >> 1)
    return v & 1


def butterflies(values):
    step = 1
    while step < len(values):
        out = list(values)
        for i in range(len(values)):
            if not i & step:
                out[i] = values[i] + values[i | step]
                out[i | step] = values[i] - values[i | step]
        values = out
        step *= 2
    return values


def halves(x):
    top = x.astype(bf16)
    return top, (x - top.astype(f32)).astype(bf16)


def transform_kernel(width, x_ref, sign_ref, mixed_ref, work_ref):
    bands = width // 8

    def first(lo, _):
        signs = [sign_ref[pl.ds(hi * 8 + lo, 1), :].astype(f32) for hi in range(16)]
        for band in range(bands):
            rows = pl.ds(band * 8, 8)
            values = []
            for hi in range(16):
                start = pl.multiple_of((hi * 8 + lo) * LANES, LANES)
                values.append(x_ref[rows, pl.ds(start, LANES)] * signs[hi])
            for hi, value in enumerate(butterflies(values)):
                work_ref[hi * 8 + lo, rows, :] = value
        return 0

    lax.fori_loop(0, 8, first, 0)
    row = lax.broadcasted_iota(jnp.int32, (LANES, 2 * LANES), 0)
    column = lax.broadcasted_iota(jnp.int32, (LANES, 2 * LANES), 1)
    hadamard = (1 - 2 * parity(row & (column & (LANES - 1)))).astype(f32).astype(bf16)
    blocks = 8 * width // LANES

    def second(hi, _):
        rows = [
            butterflies([work_ref[hi * 8 + lo, pl.ds(band * 8, 8), :] for lo in range(8)]) for band in range(bands)
        ]
        y = jnp.concatenate([rows[band][lo] for lo in range(8) for band in range(bands)], axis=0)
        both = jnp.concatenate(halves(y), axis=1)
        mixed = lax.dot_general(hadamard, both, (((1,), (1,)), ((), ())), preferred_element_type=f32)
        for block in range(blocks):
            start = pl.multiple_of((hi * blocks + block) * LANES, LANES)
            mixed_ref[pl.ds(start, LANES), :] = mixed[:, block * LANES : (block + 1) * LANES]
        return 0

    lax.fori_loop(0, 16, second, 0, unroll=4)


def table_kernel(width, mixed_ref, table_ref):
    group = LANES // width
    lane = lax.broadcasted_iota(jnp.int32, (LANES, LANES), 1) // width
    in_lane = [lane == g for g in range(group)]

    def some(block, _):
        mixed = mixed_ref[pl.ds(pl.multiple_of(block * LANES, LANES), LANES), :]
        turned = [mixed] + [pltpu.roll(mixed, k * width, 1) for k in range(1, group)]
        for e in range(group):
            total = turned[-e % group]
            for g in range(1, group):
                total = jnp.where(in_lane[g], turned[(g - e) % group], total)
            table_ref[pl.ds(pl.multiple_of((block * group + e) * LANES, LANES), LANES), :] = total
        return 0

    lax.fori_loop(0, LANES // group, some, 0, unroll=2)


def pick_kernel(width, pieces, count, straight, *refs):
    offset_refs, table_ref, out_refs = refs[: -1 - len(pieces)], refs[-1 - len(pieces)], refs[-len(pieces) :]
    group = LANES // width
    per = count // group
    lane = lax.broadcasted_iota(jnp.int32, (8, LANES), 1) // width
    sub = lax.broadcasted_iota(jnp.int32, (8, LANES), 0)
    in_sub = [sub == s for s in range(8)]
    in_lane = [lane == g for g in range(group)]
    me = lax.axis_index("row")
    for out_ref, (slots, first, rows) in zip(out_refs, pieces):
        for place, (slot, which, base) in enumerate(slots):
            sign = (1 - 2 * parity(me & (me ^ slot))).astype(f32)

            def block(inner):
                total = None
                for g in range(group):
                    part = None
                    for s in range(8):
                        spot = offset_refs[which][inner + (base + first + g * per + s)]
                        value = jnp.broadcast_to(table_ref[pl.ds(spot, 1), :], (8, LANES))
                        part = value if part is None else jnp.where(in_sub[s], value, part)
                    total = part if total is None else jnp.where(in_lane[g], part, total)
                return total * sign

            if straight:
                for inner in range(0, rows, 8):
                    out_ref[pl.ds(place * rows + inner, 8), :] = block(inner)
            else:

                def some(it, _):
                    inner = pl.multiple_of(it * 8, 8)
                    out_ref[pl.ds(place * rows + inner, 8), :] = block(inner)
                    return 0

                lax.fori_loop(0, rows // 8, some, 0)


def gram_kernel(width, count, named, scale, owner_ref, *refs):
    group = LANES // width
    per = count // group
    packed, out_ref = refs[:-1], refs[-1]
    lane = lax.broadcasted_iota(jnp.int32, (per, LANES), 1)
    parts, repeated = [], []
    for g in range(group):
        total = packed[g][...]
        for u in range(group):
            if u != g:
                moved = jnp.take_along_axis(packed[u][...], lane ^ ((u ^ g) * width), axis=1)
                total = jnp.where(lane // width == u, moved, total)
        parts.append(total)
        repeated.append(jnp.take_along_axis(packed[0][...], (lane & (width - 1)) + g * width, axis=1))
    sketch = jnp.concatenate(parts, axis=0)
    mine = jnp.concatenate(repeated, axis=0)
    top, low = halves(sketch)
    mine_top, mine_low = halves(mine)
    whose = jnp.broadcast_to(owner_ref[...], (count, LANES))
    tall = lax.broadcasted_iota(jnp.int32, (count, LANES), 1) // width
    zero = jnp.zeros((count, LANES), bf16)
    me, col = lax.axis_index("row"), lax.axis_index("col")
    turned = lax.broadcasted_iota(jnp.int32, (LANES, LANES), 1) ^ (col * width)
    over = (((0,), (0,)), ((), ()))
    for block in range(named * width // LANES):
        match = whose == tall + block * group
        left = jnp.where(match, mine_top, zero)
        gram = lax.dot_general(left, top, over, preferred_element_type=f32)
        gram = gram + lax.dot_general(left, low, over, preferred_element_type=f32)
        left = jnp.where(match, mine_low, zero)
        gram = gram + lax.dot_general(left, top, over, preferred_element_type=f32)
        gram = jnp.take_along_axis(gram, turned, axis=1) * scale
        for k in range(group):
            slot = (block * group + k) ^ me
            place = (slot & 3) * (named // 4) + (slot >> 2)
            out_ref[pl.ds(pl.multiple_of(place * width, 8), width), :] = gram[k * width : (k + 1) * width]


VMEM = pl.BlockSpec(memory_space=pltpu.VMEM)
SMEM = pl.BlockSpec(memory_space=pltpu.SMEM)
PARAMS = pltpu.CompilerParams(vmem_limit_bytes=24 << 20)


def transform(panel, signs):
    width, row_count = panel.shape
    return pl.pallas_call(
        functools.partial(transform_kernel, width),
        out_shape=jax.ShapeDtypeStruct((row_count * width // LANES, LANES), f32),
        in_specs=[VMEM] * 2,
        out_specs=VMEM,
        scratch_shapes=[pltpu.VMEM((LANES, width, LANES), f32)],
        compiler_params=PARAMS,
        name="transform",
    )(panel, signs.reshape(LANES, LANES))


def spread_lanes(mixed, width):
    return pl.pallas_call(
        functools.partial(table_kernel, width),
        out_shape=jax.ShapeDtypeStruct((LANES * LANES, LANES), f32),
        in_specs=[VMEM],
        out_specs=VMEM,
        compiler_params=PARAMS,
        name="table",
    )(mixed)


def reverse(i, bits):
    return int(format(i, f"0{bits}b")[::-1], 2) if bits else 0


def body(panel, signs, offsets, owners):
    width, row_count = panel.shape
    devices = lax.axis_size("row")
    bits = devices.bit_length() - 1
    count = offsets.shape[0]
    group = LANES // width
    per = count // group
    near = min(bits, 2)
    listed = [offsets]
    for t in range(1, 1 << near):
        listed.append(swapped(offsets, "row", t))
    mixed = transform(panel, signs)
    arrays, entries = list(listed), [(t, 0) for t in range(1 << near)]
    if bits > near:
        far = jnp.concatenate(listed)
        far = swapped(far, "row", 1 << near)
        arrays.append(far)
        entries += [(len(arrays) - 1, t * count) for t in range(1 << near)]
        for level in range(near + 1, bits):
            held = jnp.concatenate([arrays[k][at : at + count] for k, at in entries])
            arrays.append(swapped(held, "row", 1 << level))
            entries += [(len(arrays) - 1, t * count) for t in range(1 << level)]
    table = spread_lanes(mixed, width)

    def pick(*pieces):
        used = sorted({entries[t][0] for slots, _, _ in pieces for t in slots})
        full = [
            ([(t, used.index(entries[t][0]), entries[t][1]) for t in slots], first, rows)
            for slots, first, rows in pieces
        ]
        straight = sum(len(slots) * rows for slots, _, rows in pieces) * group <= 4096
        return pl.pallas_call(
            functools.partial(pick_kernel, width, full, count, straight),
            out_shape=[jax.ShapeDtypeStruct((len(slots) * rows, LANES), f32) for slots, _, rows in pieces],
            in_specs=[SMEM] * len(used) + [VMEM],
            out_specs=[VMEM] * len(pieces),
            compiler_params=PARAMS,
            name="pick",
        )(*[arrays[k] for k in used], table)

    def split(slots, levels):
        slots = sorted(slots, key=lambda t: [t >> level & 1 for level in levels])
        return slots[: len(slots) // 2], slots[len(slots) // 2 :]

    levels = list(range(bits - 1))
    half = per // 2
    keep_up, send_up = split(range(devices // 2, devices), levels)
    keep_low, send_low = split(range(devices // 2), levels)
    sent, kept = [None] * 3, [None] * 3
    sent[0], sent[1] = pick((send_up, 0, half), (send_up, half, half))
    sent[2], kept[0], kept[1] = pick((send_low, 0, per), (keep_up, 0, half), (keep_up, half, half))
    (kept[2],) = pick((keep_low, 0, per))
    totals = []
    for k in range(3):
        total, out = kept[k], sent[k]
        for step, level in enumerate(levels):
            if step:
                middle = total.shape[0] // 2
                total, out = total[:middle], total[middle:]
            other = swapped(out, "row", 1 << level)
            total = total + other
        totals.append(total)
    col_size = lax.axis_size("col")
    col_bits = col_size.bit_length() - 1
    own, other = [], []
    for part in range(2):
        mine = totals[2][part * per // 2 : (part + 1) * per // 2]
        if part:
            mine, own[0] = lax.optimization_barrier((mine, own[0]))
        own.append(mine + swapped(totals[part], "row", devices // 2))
        other.append(swapped(own[part], "col", col_size // 2))
    stacked = jnp.stack([jnp.concatenate(own), jnp.concatenate(other)])
    for level in reversed(range(col_bits - 1)):
        stacked = jnp.concatenate([stacked, swapped(stacked, "col", 1 << level)], axis=0)
    packed = [stacked[reverse(u, col_bits)] for u in range(group)]
    scale = 1.0 / (devices * row_count * count)
    gram = pl.pallas_call(
        functools.partial(gram_kernel, width, count, devices, scale),
        out_shape=jax.ShapeDtypeStruct((devices * width, LANES), f32),
        in_specs=[VMEM] * (1 + group),
        out_specs=VMEM,
        compiler_params=PARAMS,
        name="gram",
    )(owners, *packed)
    gram = gram.reshape(1 << near, devices >> near, width, LANES)
    total = gram[0]
    for t in range(1, 1 << near):
        total = total + swapped(gram[t], "row", t)
    for level in reversed(range(near, bits)):
        middle = total.shape[0] // 2
        total = total[:middle] + swapped(total[middle:], "row", 1 << level)
    return total


def solution(mesh):
    placed = (P("col", "row"), P("row"), P("row"), P("row", None))
    return jax.shard_map(body, mesh=mesh, in_specs=placed, out_specs=P("row", "col", None), check_vma=False)
```

```python
import functools

import jax
import jax.numpy as jnp
from jax import lax
from jax.experimental import pallas as pl
from jax.experimental.pallas import tpu as pltpu
from jax.sharding import PartitionSpec as P


LANES = 128
f32, bf16 = jnp.float32, jnp.bfloat16


def swapped(x, axis, distance):
    return lax.ppermute(x, axis, [(i, i ^ distance) for i in range(lax.axis_size(axis))])


def parity(v):
    v = v ^ (v >> 8)
    v = v ^ (v >> 4)
    v = v ^ (v >> 2)
    v = v ^ (v >> 1)
    return v & 1


def butterflies(values):
    step = 1
    while step < len(values):
        out = list(values)
        for i in range(len(values)):
            if not i & step:
                out[i] = values[i] + values[i | step]
                out[i | step] = values[i] - values[i | step]
        values = out
        step *= 2
    return values


def halves(x):
    top = x.astype(bf16)
    return top, (x - top.astype(f32)).astype(bf16)


def signs_of(rows, columns):
    row = lax.broadcasted_iota(jnp.int32, (rows, columns), 0)
    column = lax.broadcasted_iota(jnp.int32, (rows, columns), 1)
    return (1 - 2 * parity(row & (column & (LANES - 1)))).astype(f32).astype(bf16)


def times(hadamard, both):
    return lax.dot_general(hadamard, both, (((1,), (1,)), ((), ())), preferred_element_type=f32)


def transform_kernel(width, rolled, x_ref, sign_ref, both_ref, mixed_ref, work_ref):
    bands = width // 8

    def first(lo, _):
        signs = [sign_ref[pl.ds(hi * 8 + lo, 1), :].astype(f32) for hi in range(16)]
        for band in range(bands):
            rows = pl.ds(band * 8, 8)
            values = []
            for hi in range(16):
                start = pl.multiple_of((hi * 8 + lo) * LANES, LANES)
                values.append(x_ref[rows, pl.ds(start, LANES)] * signs[hi])
            for hi, value in enumerate(butterflies(values)):
                work_ref[hi * 8 + lo, rows, :] = value
        return 0

    lax.fori_loop(0, 8, first, 0)
    hadamard = signs_of(LANES, 2 * LANES)
    straight = (8 - rolled) * width

    def second(hi, _):
        rows = [
            butterflies([work_ref[hi * 8 + lo, pl.ds(band * 8, 8), :] for lo in range(8)]) for band in range(bands)
        ]
        y = jnp.concatenate([rows[band][lo] for lo in range(8) for band in range(bands)], axis=0)
        both = jnp.concatenate(halves(y), axis=1)
        both_ref[pl.ds(pl.multiple_of(hi * straight, 8), straight), :] = both[:straight]
        if rolled:
            mixed_ref[pl.ds(pl.multiple_of(hi * LANES, LANES), LANES), :] = times(hadamard, both[straight:])
        return 0

    lax.fori_loop(0, 16, second, 0, unroll=4)


def table_kernel(width, rolled, both_ref, mixed_ref, table_ref):
    group = LANES // width
    lane = lax.broadcasted_iota(jnp.int32, (LANES, LANES), 1) // width
    in_lane = [lane == g for g in range(group)]
    hadamard = signs_of(LANES, 2 * LANES)
    straight = (8 - rolled) * width

    def some(hi, _):
        results = []
        for e in range(0, 8 - rolled, 2):
            rows = [both_ref[pl.ds(hi * straight + (e + i) * width, width), :] for i in range(2)]
            mixed = times(hadamard, jnp.concatenate([row for row in rows for _ in range(group)], axis=0))
            results += [mixed[:, :LANES], mixed[:, LANES:]]
        if rolled:
            mixed = mixed_ref[pl.ds(pl.multiple_of(hi * LANES, LANES), LANES), :]
            turned = [mixed] + [pltpu.roll(mixed, k * width, 1) for k in range(1, group)]
            for e in range(group):
                total = turned[-e % group]
                for g in range(1, group):
                    total = jnp.where(in_lane[g], turned[(g - e) % group], total)
                results.append(total)
        for e, result in enumerate(results):
            table_ref[pl.ds(pl.multiple_of((hi * 8 + e) * LANES, LANES), LANES), :] = result
        return 0

    lax.fori_loop(0, 16, some, 0, unroll=4)


def pick_kernel(width, pieces, count, straight, *refs):
    offset_refs, table_ref, out_refs = refs[: -1 - len(pieces)], refs[-1 - len(pieces)], refs[-len(pieces) :]
    group = LANES // width
    per = count // group
    lane = lax.broadcasted_iota(jnp.int32, (8, LANES), 1) // width
    sub = lax.broadcasted_iota(jnp.int32, (8, LANES), 0)
    in_sub = [sub == s for s in range(8)]
    in_lane = [lane == g for g in range(group)]
    me = lax.axis_index("row")
    for out_ref, (slots, first, rows) in zip(out_refs, pieces):
        for place, (slot, which, base) in enumerate(slots):
            sign = (1 - 2 * parity(me & (me ^ slot))).astype(f32)

            def block(inner):
                total = None
                for g in range(group):
                    part = None
                    for s in range(8):
                        spot = offset_refs[which][inner + (base + first + g * per + s)]
                        value = jnp.broadcast_to(table_ref[pl.ds(spot, 1), :], (8, LANES))
                        part = value if part is None else jnp.where(in_sub[s], value, part)
                    total = part if total is None else jnp.where(in_lane[g], part, total)
                return total * sign

            if straight:
                for inner in range(0, rows, 8):
                    out_ref[pl.ds(place * rows + inner, 8), :] = block(inner)
            else:

                def some(it, _):
                    inner = pl.multiple_of(it * 8, 8)
                    out_ref[pl.ds(place * rows + inner, 8), :] = block(inner)
                    return 0

                lax.fori_loop(0, rows // 8, some, 0)


def gram_kernel(width, count, named, scale, owner_ref, *refs):
    group = LANES // width
    per = count // group
    packed, out_ref = refs[:-1], refs[-1]
    lane = lax.broadcasted_iota(jnp.int32, (per, LANES), 1)
    in_lane = [lane // width == u for u in range(group)]
    turned = [[ref[...]] + [pltpu.roll(ref[...], k * width, 1) for k in range(1, group)] for ref in packed]
    parts, repeated = [], []
    for g in range(group):
        total, mine = turned[0][-g % group], turned[0][-g % group]
        for u in range(1, group):
            total = jnp.where(in_lane[u], turned[u][(u - g) % group], total)
            mine = jnp.where(in_lane[u], turned[0][(u - g) % group], mine)
        parts.append(total)
        repeated.append(mine)
    sketch = jnp.concatenate(parts, axis=0)
    mine = jnp.concatenate(repeated, axis=0)
    top, low = halves(sketch)
    mine_top, mine_low = halves(mine)
    whose = jnp.broadcast_to(owner_ref[...], (count, LANES))
    tall = lax.broadcasted_iota(jnp.int32, (count, LANES), 1) // width
    zero = jnp.zeros((count, LANES), bf16)
    me, col = lax.axis_index("row"), lax.axis_index("col")
    turned = lax.broadcasted_iota(jnp.int32, (LANES, LANES), 1) ^ (col * width)
    over = (((0,), (0,)), ((), ()))
    for block in range(named * width // LANES):
        match = whose == tall + block * group
        left = jnp.where(match, mine_top, zero)
        gram = lax.dot_general(left, top, over, preferred_element_type=f32)
        gram = gram + lax.dot_general(left, low, over, preferred_element_type=f32)
        left = jnp.where(match, mine_low, zero)
        gram = gram + lax.dot_general(left, top, over, preferred_element_type=f32)
        gram = jnp.take_along_axis(gram, turned, axis=1) * scale
        for k in range(group):
            slot = (block * group + k) ^ me
            place = (slot & 3) * (named // 4) + (slot >> 2)
            out_ref[pl.ds(pl.multiple_of(place * width, 8), width), :] = gram[k * width : (k + 1) * width]


VMEM = pl.BlockSpec(memory_space=pltpu.VMEM)
SMEM = pl.BlockSpec(memory_space=pltpu.SMEM)
PARAMS = pltpu.CompilerParams(vmem_limit_bytes=24 << 20)


def transform(panel, signs):
    width, _ = panel.shape
    rolled = LANES // width if 8 * width > LANES else 0
    return pl.pallas_call(
        functools.partial(transform_kernel, width, rolled),
        out_shape=[
            jax.ShapeDtypeStruct((16 * (8 - rolled) * width, 2 * LANES), bf16),
            jax.ShapeDtypeStruct((16 * LANES, LANES), f32),
        ],
        in_specs=[VMEM] * 2,
        out_specs=[VMEM] * 2,
        scratch_shapes=[pltpu.VMEM((LANES, width, LANES), f32)],
        compiler_params=PARAMS,
        name="transform",
    )(panel, signs.reshape(LANES, LANES))


def spread_lanes(parts, width):
    rolled = LANES // width if 8 * width > LANES else 0
    return pl.pallas_call(
        functools.partial(table_kernel, width, rolled),
        out_shape=jax.ShapeDtypeStruct((LANES * LANES, LANES), f32),
        in_specs=[VMEM] * 2,
        out_specs=VMEM,
        compiler_params=PARAMS,
        name="table",
    )(*parts)


def reverse(i, bits):
    return int(format(i, f"0{bits}b")[::-1], 2) if bits else 0


def body(panel, signs, offsets, owners):
    width, row_count = panel.shape
    devices = lax.axis_size("row")
    bits = devices.bit_length() - 1
    count = offsets.shape[0]
    group = LANES // width
    per = count // group
    near = min(bits, 2)
    listed = [offsets]
    for t in range(1, 1 << near):
        listed.append(swapped(offsets, "row", t))
    parts = transform(panel, signs)
    arrays, entries = list(listed), [(t, 0) for t in range(1 << near)]
    if bits > near:
        far = jnp.concatenate(listed)
        far = swapped(far, "row", 1 << near)
        arrays.append(far)
        entries += [(len(arrays) - 1, t * count) for t in range(1 << near)]
        for level in range(near + 1, bits):
            held = jnp.concatenate([arrays[k][at : at + count] for k, at in entries])
            arrays.append(swapped(held, "row", 1 << level))
            entries += [(len(arrays) - 1, t * count) for t in range(1 << level)]
    table = spread_lanes(parts, width)

    def pick(*pieces):
        used = sorted({entries[t][0] for slots, _, _ in pieces for t in slots})
        full = [
            ([(t, used.index(entries[t][0]), entries[t][1]) for t in slots], first, rows)
            for slots, first, rows in pieces
        ]
        straight = sum(len(slots) * rows for slots, _, rows in pieces) * group <= 4096
        return pl.pallas_call(
            functools.partial(pick_kernel, width, full, count, straight),
            out_shape=[jax.ShapeDtypeStruct((len(slots) * rows, LANES), f32) for slots, _, rows in pieces],
            in_specs=[SMEM] * len(used) + [VMEM],
            out_specs=[VMEM] * len(pieces),
            compiler_params=PARAMS,
            name="pick",
        )(*[arrays[k] for k in used], table)

    def split(slots, levels):
        slots = sorted(slots, key=lambda t: [t >> level & 1 for level in levels])
        return slots[: len(slots) // 2], slots[len(slots) // 2 :]

    levels = list(range(bits - 1))
    half = per // 2
    keep_up, send_up = split(range(devices // 2, devices), levels)
    keep_low, send_low = split(range(devices // 2), levels)
    sent, kept = [None] * 3, [None] * 3
    sent[0], sent[1] = pick((send_up, 0, half), (send_up, half, half))
    sent[2], kept[0], kept[1] = pick((send_low, 0, per), (keep_up, 0, half), (keep_up, half, half))
    (kept[2],) = pick((keep_low, 0, per))
    totals = []
    for k in range(3):
        total, out = kept[k], sent[k]
        for step, level in enumerate(levels):
            if step:
                middle = total.shape[0] // 2
                total, out = total[:middle], total[middle:]
            other = swapped(out, "row", 1 << level)
            total = total + other
        totals.append(total)
    col_size = lax.axis_size("col")
    col_bits = col_size.bit_length() - 1
    own, other = [], []
    for part in range(2):
        mine = totals[2][part * per // 2 : (part + 1) * per // 2]
        if part:
            mine, own[0] = lax.optimization_barrier((mine, own[0]))
        own.append(mine + swapped(totals[part], "row", devices // 2))
        other.append(swapped(own[part], "col", col_size // 2))
    stacked = jnp.stack([jnp.concatenate(own), jnp.concatenate(other)])
    for level in reversed(range(col_bits - 1)):
        stacked = jnp.concatenate([stacked, swapped(stacked, "col", 1 << level)], axis=0)
    packed = [stacked[reverse(u, col_bits)] for u in range(group)]
    scale = 1.0 / (devices * row_count * count)
    gram = pl.pallas_call(
        functools.partial(gram_kernel, width, count, devices, scale),
        out_shape=jax.ShapeDtypeStruct((devices * width, LANES), f32),
        in_specs=[VMEM] * (1 + group),
        out_specs=VMEM,
        compiler_params=PARAMS,
        name="gram",
    )(owners, *packed)
    gram = gram.reshape(1 << near, devices >> near, width, LANES)
    total = gram[0]
    for t in range(1, 1 << near):
        total = total + swapped(gram[t], "row", t)
    for level in reversed(range(near, bits)):
        middle = total.shape[0] // 2
        total = total[:middle] + swapped(total[middle:], "row", 1 << level)
    return total


def solution(mesh):
    placed = (P("col", "row"), P("row"), P("row"), P("row", None))
    return jax.shard_map(body, mesh=mesh, in_specs=placed, out_specs=P("row", "col", None), check_vma=False)
```

```python
import functools

import jax
import jax.numpy as jnp
from jax import lax
from jax.experimental import pallas as pl
from jax.experimental.pallas import tpu as pltpu
from jax.sharding import PartitionSpec as P


LANES = 128
f32, bf16 = jnp.float32, jnp.bfloat16


def swapped(x, axis, distance):
    return lax.ppermute(x, axis, [(i, i ^ distance) for i in range(lax.axis_size(axis))])


def parity(v):
    v = v ^ (v >> 8)
    v = v ^ (v >> 4)
    v = v ^ (v >> 2)
    v = v ^ (v >> 1)
    return v & 1


def butterflies(values):
    step = 1
    while step < len(values):
        out = list(values)
        for i in range(len(values)):
            if not i & step:
                out[i] = values[i] + values[i | step]
                out[i | step] = values[i] - values[i | step]
        values = out
        step *= 2
    return values


def halves(x):
    top = x.astype(bf16)
    return top, (x - top.astype(f32)).astype(bf16)


def signs_of(rows, columns):
    row = lax.broadcasted_iota(jnp.int32, (rows, columns), 0)
    column = lax.broadcasted_iota(jnp.int32, (rows, columns), 1)
    return (1 - 2 * parity(row & (column & (LANES - 1)))).astype(f32).astype(bf16)


def times(hadamard, both):
    return lax.dot_general(hadamard, both, (((1,), (1,)), ((), ())), preferred_element_type=f32)


def transform_kernel(width, x_ref, sign_ref, both_ref, work_ref):
    bands = width // 8

    def first(lo, _):
        signs = [sign_ref[pl.ds(hi * 8 + lo, 1), :].astype(f32) for hi in range(16)]
        for band in range(bands):
            rows = pl.ds(band * 8, 8)
            values = []
            for hi in range(16):
                start = pl.multiple_of((hi * 8 + lo) * LANES, LANES)
                values.append(x_ref[rows, pl.ds(start, LANES)] * signs[hi])
            for hi, value in enumerate(butterflies(values)):
                work_ref[hi * 8 + lo, rows, :] = value
        return 0

    lax.fori_loop(0, 8, first, 0)

    def second(hi, _):
        rows = [
            butterflies([work_ref[hi * 8 + lo, pl.ds(band * 8, 8), :] for lo in range(8)]) for band in range(bands)
        ]
        y = jnp.concatenate([rows[band][lo] for lo in range(8) for band in range(bands)], axis=0)
        both = jnp.concatenate(halves(y), axis=1)
        both_ref[pl.ds(pl.multiple_of(hi * 8 * width, LANES), 8 * width), :] = both
        return 0

    lax.fori_loop(0, 16, second, 0, unroll=4)


def table_kernel(width, rolled, both_ref, table_ref):
    group = LANES // width
    lane = lax.broadcasted_iota(jnp.int32, (LANES, LANES), 1) // width
    in_lane = [lane == g for g in range(group)]
    hadamard = signs_of(LANES, 2 * LANES)

    def some(hi, _):
        top = pl.multiple_of(hi * 8 * width, LANES)
        results = []
        for e in range(0, 8 - rolled, 2):
            rows = [both_ref[pl.ds(top + (e + i) * width, width), :] for i in range(2)]
            mixed = times(hadamard, jnp.concatenate([row for row in rows for _ in range(group)], axis=0))
            results += [mixed[:, :LANES], mixed[:, LANES:]]
        if rolled:
            mixed = times(hadamard, both_ref[pl.ds(top + (8 - rolled) * width, LANES), :])
            turned = [mixed] + [pltpu.roll(mixed, k * width, 1) for k in range(1, group)]
            for e in range(group):
                total = turned[-e % group]
                for g in range(1, group):
                    total = jnp.where(in_lane[g], turned[(g - e) % group], total)
                results.append(total)
        for e, result in enumerate(results):
            table_ref[pl.ds(pl.multiple_of((hi * 8 + e) * LANES, LANES), LANES), :] = result
        return 0

    lax.fori_loop(0, 16, some, 0, unroll=4)


def pick_kernel(width, pieces, count, straight, *refs):
    offset_refs, table_ref, out_refs = refs[: -1 - len(pieces)], refs[-1 - len(pieces)], refs[-len(pieces) :]
    group = LANES // width
    per = count // group
    lane = lax.broadcasted_iota(jnp.int32, (8, LANES), 1) // width
    sub = lax.broadcasted_iota(jnp.int32, (8, LANES), 0)
    in_sub = [sub == s for s in range(8)]
    in_lane = [lane == g for g in range(group)]
    me = lax.axis_index("row")
    for out_ref, (slots, first, rows) in zip(out_refs, pieces):
        for place, (slot, which, base) in enumerate(slots):
            sign = (1 - 2 * parity(me & (me ^ slot))).astype(f32)

            def block(inner):
                total = None
                for g in range(group):
                    part = None
                    for s in range(8):
                        spot = offset_refs[which][inner + (base + first + g * per + s)]
                        value = jnp.broadcast_to(table_ref[pl.ds(spot, 1), :], (8, LANES))
                        part = value if part is None else jnp.where(in_sub[s], value, part)
                    total = part if total is None else jnp.where(in_lane[g], part, total)
                return total * sign

            if straight:
                for inner in range(0, rows, 8):
                    out_ref[pl.ds(place * rows + inner, 8), :] = block(inner)
            else:

                def some(it, _):
                    inner = pl.multiple_of(it * 8, 8)
                    out_ref[pl.ds(place * rows + inner, 8), :] = block(inner)
                    return 0

                lax.fori_loop(0, rows // 8, some, 0)


def gram_kernel(width, count, named, scale, owner_ref, *refs):
    group = LANES // width
    per = count // group
    packed, out_ref = refs[:-1], refs[-1]
    lane = lax.broadcasted_iota(jnp.int32, (per, LANES), 1)
    in_lane = [lane // width == u for u in range(group)]
    turned = [[ref[...]] + [pltpu.roll(ref[...], k * width, 1) for k in range(1, group)] for ref in packed]
    parts, repeated = [], []
    for g in range(group):
        total, mine = turned[0][-g % group], turned[0][-g % group]
        for u in range(1, group):
            total = jnp.where(in_lane[u], turned[u][(u - g) % group], total)
            mine = jnp.where(in_lane[u], turned[0][(u - g) % group], mine)
        parts.append(total)
        repeated.append(mine)
    sketch = jnp.concatenate(parts, axis=0)
    mine = jnp.concatenate(repeated, axis=0)
    top, low = halves(sketch)
    mine_top, mine_low = halves(mine)
    whose = jnp.broadcast_to(owner_ref[...], (count, LANES))
    tall = lax.broadcasted_iota(jnp.int32, (count, LANES), 1) // width
    zero = jnp.zeros((count, LANES), bf16)
    me, col = lax.axis_index("row"), lax.axis_index("col")
    turned = lax.broadcasted_iota(jnp.int32, (LANES, LANES), 1) ^ (col * width)
    over = (((0,), (0,)), ((), ()))
    for block in range(named * width // LANES):
        match = whose == tall + block * group
        left = jnp.where(match, mine_top, zero)
        gram = lax.dot_general(left, top, over, preferred_element_type=f32)
        gram = gram + lax.dot_general(left, low, over, preferred_element_type=f32)
        left = jnp.where(match, mine_low, zero)
        gram = gram + lax.dot_general(left, top, over, preferred_element_type=f32)
        gram = jnp.take_along_axis(gram, turned, axis=1) * scale
        for k in range(group):
            slot = (block * group + k) ^ me
            place = (slot & 3) * (named // 4) + (slot >> 2)
            out_ref[pl.ds(pl.multiple_of(place * width, 8), width), :] = gram[k * width : (k + 1) * width]


VMEM = pl.BlockSpec(memory_space=pltpu.VMEM)
SMEM = pl.BlockSpec(memory_space=pltpu.SMEM)
PARAMS = pltpu.CompilerParams(vmem_limit_bytes=24 << 20)


def transform(panel, signs):
    width, _ = panel.shape
    return pl.pallas_call(
        functools.partial(transform_kernel, width),
        out_shape=jax.ShapeDtypeStruct((LANES * width, 2 * LANES), bf16),
        in_specs=[VMEM] * 2,
        out_specs=VMEM,
        scratch_shapes=[pltpu.VMEM((LANES, width, LANES), f32)],
        compiler_params=PARAMS,
        name="transform",
    )(panel, signs.reshape(LANES, LANES))


def spread_lanes(parts, width):
    rolled = LANES // width if 8 * width > LANES else 0
    return pl.pallas_call(
        functools.partial(table_kernel, width, rolled),
        out_shape=jax.ShapeDtypeStruct((LANES * LANES, LANES), f32),
        in_specs=[VMEM],
        out_specs=VMEM,
        compiler_params=PARAMS,
        name="table",
    )(parts)


def reverse(i, bits):
    return int(format(i, f"0{bits}b")[::-1], 2) if bits else 0


def body(panel, signs, offsets, owners):
    width, row_count = panel.shape
    devices = lax.axis_size("row")
    bits = devices.bit_length() - 1
    count = offsets.shape[0]
    group = LANES // width
    per = count // group
    near = min(bits, 2)
    listed = [offsets]
    for t in range(1, 1 << near):
        listed.append(swapped(offsets, "row", t))
    parts = transform(panel, signs)
    arrays, entries = list(listed), [(t, 0) for t in range(1 << near)]
    if bits > near:
        far = jnp.concatenate(listed)
        far = swapped(far, "row", 1 << near)
        arrays.append(far)
        entries += [(len(arrays) - 1, t * count) for t in range(1 << near)]
        for level in range(near + 1, bits):
            held = jnp.concatenate([arrays[k][at : at + count] for k, at in entries])
            arrays.append(swapped(held, "row", 1 << level))
            entries += [(len(arrays) - 1, t * count) for t in range(1 << level)]
    table = spread_lanes(parts, width)

    def pick(*pieces):
        used = sorted({entries[t][0] for slots, _, _ in pieces for t in slots})
        full = [
            ([(t, used.index(entries[t][0]), entries[t][1]) for t in slots], first, rows)
            for slots, first, rows in pieces
        ]
        straight = sum(len(slots) * rows for slots, _, rows in pieces) * group <= 4096
        return pl.pallas_call(
            functools.partial(pick_kernel, width, full, count, straight),
            out_shape=[jax.ShapeDtypeStruct((len(slots) * rows, LANES), f32) for slots, _, rows in pieces],
            in_specs=[SMEM] * len(used) + [VMEM],
            out_specs=[VMEM] * len(pieces),
            compiler_params=PARAMS,
            name="pick",
        )(*[arrays[k] for k in used], table)

    def split(slots, levels):
        slots = sorted(slots, key=lambda t: [t >> level & 1 for level in levels])
        return slots[: len(slots) // 2], slots[len(slots) // 2 :]

    levels = list(range(bits - 1))
    half = per // 2
    keep_up, send_up = split(range(devices // 2, devices), levels)
    keep_low, send_low = split(range(devices // 2), levels)
    sent, kept = [None] * 3, [None] * 3
    sent[0], sent[1] = pick((send_up, 0, half), (send_up, half, half))
    sent[2], kept[0], kept[1] = pick((send_low, 0, per), (keep_up, 0, half), (keep_up, half, half))
    (kept[2],) = pick((keep_low, 0, per))
    totals = []
    for k in range(3):
        total, out = kept[k], sent[k]
        for step, level in enumerate(levels):
            if step:
                middle = total.shape[0] // 2
                total, out = total[:middle], total[middle:]
            other = swapped(out, "row", 1 << level)
            total = total + other
        totals.append(total)
    col_size = lax.axis_size("col")
    col_bits = col_size.bit_length() - 1
    own, other = [], []
    for part in range(2):
        mine = totals[2][part * per // 2 : (part + 1) * per // 2]
        if part:
            mine, own[0] = lax.optimization_barrier((mine, own[0]))
        own.append(mine + swapped(totals[part], "row", devices // 2))
        other.append(swapped(own[part], "col", col_size // 2))
    stacked = jnp.stack([jnp.concatenate(own), jnp.concatenate(other)])
    for level in reversed(range(col_bits - 1)):
        stacked = jnp.concatenate([stacked, swapped(stacked, "col", 1 << level)], axis=0)
    packed = [stacked[reverse(u, col_bits)] for u in range(group)]
    scale = 1.0 / (devices * row_count * count)
    gram = pl.pallas_call(
        functools.partial(gram_kernel, width, count, devices, scale),
        out_shape=jax.ShapeDtypeStruct((devices * width, LANES), f32),
        in_specs=[VMEM] * (1 + group),
        out_specs=VMEM,
        compiler_params=PARAMS,
        name="gram",
    )(owners, *packed)
    gram = gram.reshape(1 << near, devices >> near, width, LANES)
    total = gram[0]
    for t in range(1, 1 << near):
        total = total + swapped(gram[t], "row", t)
    for level in reversed(range(near, bits)):
        middle = total.shape[0] // 2
        total = total[:middle] + swapped(total[middle:], "row", 1 << level)
    return total


def solution(mesh):
    placed = (P("col", "row"), P("row"), P("row"), P("row", None))
    return jax.shard_map(body, mesh=mesh, in_specs=placed, out_specs=P("row", "col", None), check_vma=False)
```

```python
import functools

import jax
import jax.numpy as jnp
from jax import lax
from jax.experimental import pallas as pl
from jax.experimental.pallas import tpu as pltpu
from jax.sharding import PartitionSpec as P


LANES = 128
f32, bf16 = jnp.float32, jnp.bfloat16


def swapped(x, axis, distance):
    return lax.ppermute(x, axis, [(i, i ^ distance) for i in range(lax.axis_size(axis))])


def parity(v):
    v = v ^ (v >> 8)
    v = v ^ (v >> 4)
    v = v ^ (v >> 2)
    v = v ^ (v >> 1)
    return v & 1


def butterflies(values):
    step = 1
    while step < len(values):
        out = list(values)
        for i in range(len(values)):
            if not i & step:
                out[i] = values[i] + values[i | step]
                out[i | step] = values[i] - values[i | step]
        values = out
        step *= 2
    return values


def halves(x):
    top = x.astype(bf16)
    return top, (x - top.astype(f32)).astype(bf16)


def signs_of(rows, columns):
    row = lax.broadcasted_iota(jnp.int32, (rows, columns), 0)
    column = lax.broadcasted_iota(jnp.int32, (rows, columns), 1)
    return (1 - 2 * parity(row & (column & (LANES - 1)))).astype(f32).astype(bf16)


def times(hadamard, both):
    return lax.dot_general(hadamard, both, (((1,), (1,)), ((), ())), preferred_element_type=f32)


def transform_kernel(width, rolled, x_ref, sign_ref, part_ref, work_ref):
    bands = width // 8

    def first(lo, _):
        signs = [sign_ref[pl.ds(hi * 8 + lo, 1), :].astype(f32) for hi in range(16)]
        for band in range(bands):
            rows = pl.ds(band * 8, 8)
            values = []
            for hi in range(16):
                start = pl.multiple_of((hi * 8 + lo) * LANES, LANES)
                values.append(x_ref[rows, pl.ds(start, LANES)] * signs[hi])
            for hi, value in enumerate(butterflies(values)):
                work_ref[hi * 8 + lo, rows, :] = value
        return 0

    lax.fori_loop(0, 8, first, 0)
    hadamard = signs_of(LANES, 2 * LANES)
    straight = (8 - rolled) * width

    def second(hi, _):
        rows = [
            butterflies([work_ref[hi * 8 + lo, pl.ds(band * 8, 8), :] for lo in range(8)]) for band in range(bands)
        ]
        y = jnp.concatenate([rows[band][lo] for lo in range(8) for band in range(bands)], axis=0)
        top = pl.multiple_of(hi * 8 * width, LANES)
        part_ref[pl.ds(top, straight), :] = y[:straight]
        if rolled:
            both = jnp.concatenate(halves(y[straight:]), axis=1)
            part_ref[pl.ds(top + straight, LANES), :] = times(hadamard, both)
        return 0

    lax.fori_loop(0, 16, second, 0, unroll=4)


def table_kernel(width, rolled, part_ref, table_ref):
    group = LANES // width
    lane = lax.broadcasted_iota(jnp.int32, (LANES, LANES), 1) // width
    in_lane = [lane == g for g in range(group)]
    hadamard = signs_of(LANES, 2 * LANES)

    def some(hi, _):
        top = pl.multiple_of(hi * 8 * width, LANES)
        results = []
        for e in range(0, 8 - rolled, 2):
            rows = [
                jnp.concatenate(halves(part_ref[pl.ds(top + (e + i) * width, width), :]), axis=1) for i in range(2)
            ]
            mixed = times(hadamard, jnp.concatenate([row for row in rows for _ in range(group)], axis=0))
            results += [mixed[:, :LANES], mixed[:, LANES:]]
        if rolled:
            mixed = part_ref[pl.ds(top + (8 - rolled) * width, LANES), :]
            turned = [mixed] + [pltpu.roll(mixed, k * width, 1) for k in range(1, group)]
            for e in range(group):
                total = turned[-e % group]
                for g in range(1, group):
                    total = jnp.where(in_lane[g], turned[(g - e) % group], total)
                results.append(total)
        for e, result in enumerate(results):
            table_ref[pl.ds(pl.multiple_of((hi * 8 + e) * LANES, LANES), LANES), :] = result
        return 0

    lax.fori_loop(0, 16, some, 0, unroll=4)


def pick_kernel(width, pieces, count, straight, *refs):
    offset_refs, table_ref, out_refs = refs[: -1 - len(pieces)], refs[-1 - len(pieces)], refs[-len(pieces) :]
    group = LANES // width
    per = count // group
    lane = lax.broadcasted_iota(jnp.int32, (8, LANES), 1) // width
    sub = lax.broadcasted_iota(jnp.int32, (8, LANES), 0)
    in_sub = [sub == s for s in range(8)]
    in_lane = [lane == g for g in range(group)]
    me = lax.axis_index("row")
    for out_ref, (slots, first, rows) in zip(out_refs, pieces):
        for place, (slot, which, base) in enumerate(slots):
            sign = (1 - 2 * parity(me & (me ^ slot))).astype(f32)

            def block(inner):
                total = None
                for g in range(group):
                    part = None
                    for s in range(8):
                        spot = offset_refs[which][inner + (base + first + g * per + s)]
                        value = jnp.broadcast_to(table_ref[pl.ds(spot, 1), :], (8, LANES))
                        part = value if part is None else jnp.where(in_sub[s], value, part)
                    total = part if total is None else jnp.where(in_lane[g], part, total)
                return total * sign

            if straight:
                for inner in range(0, rows, 8):
                    out_ref[pl.ds(place * rows + inner, 8), :] = block(inner)
            else:

                def some(it, _):
                    inner = pl.multiple_of(it * 8, 8)
                    out_ref[pl.ds(place * rows + inner, 8), :] = block(inner)
                    return 0

                lax.fori_loop(0, rows // 8, some, 0)


def gram_kernel(width, count, named, scale, owner_ref, *refs):
    group = LANES // width
    per = count // group
    packed, out_ref = refs[:-1], refs[-1]
    lane = lax.broadcasted_iota(jnp.int32, (per, LANES), 1)
    in_lane = [lane // width == u for u in range(group)]
    turned = [[ref[...]] + [pltpu.roll(ref[...], k * width, 1) for k in range(1, group)] for ref in packed]
    parts, repeated = [], []
    for g in range(group):
        total, mine = turned[0][-g % group], turned[0][-g % group]
        for u in range(1, group):
            total = jnp.where(in_lane[u], turned[u][(u - g) % group], total)
            mine = jnp.where(in_lane[u], turned[0][(u - g) % group], mine)
        parts.append(total)
        repeated.append(mine)
    sketch = jnp.concatenate(parts, axis=0)
    mine = jnp.concatenate(repeated, axis=0)
    top, low = halves(sketch)
    mine_top, mine_low = halves(mine)
    whose = jnp.broadcast_to(owner_ref[...], (count, LANES))
    tall = lax.broadcasted_iota(jnp.int32, (count, LANES), 1) // width
    zero = jnp.zeros((count, LANES), bf16)
    me, col = lax.axis_index("row"), lax.axis_index("col")
    turned = lax.broadcasted_iota(jnp.int32, (LANES, LANES), 1) ^ (col * width)
    over = (((0,), (0,)), ((), ()))
    for block in range(named * width // LANES):
        match = whose == tall + block * group
        left = jnp.where(match, mine_top, zero)
        gram = lax.dot_general(top, left, over, preferred_element_type=f32)
        gram = gram + lax.dot_general(low, left, over, preferred_element_type=f32)
        left = jnp.where(match, mine_low, zero)
        gram = (gram + lax.dot_general(top, left, over, preferred_element_type=f32)).T
        gram = jnp.take_along_axis(gram, turned, axis=1) * scale
        for k in range(group):
            slot = (block * group + k) ^ me
            place = (slot & 3) * (named // 4) + (slot >> 2)
            out_ref[pl.ds(pl.multiple_of(place * width, 8), width), :] = gram[k * width : (k + 1) * width]


VMEM = pl.BlockSpec(memory_space=pltpu.VMEM)
SMEM = pl.BlockSpec(memory_space=pltpu.SMEM)
PARAMS = pltpu.CompilerParams(vmem_limit_bytes=24 << 20)


def transform(panel, signs):
    width, _ = panel.shape
    rolled = LANES // width if 8 * width > LANES else 0
    return pl.pallas_call(
        functools.partial(transform_kernel, width, rolled),
        out_shape=jax.ShapeDtypeStruct((LANES * width, LANES), f32),
        in_specs=[VMEM] * 2,
        out_specs=VMEM,
        scratch_shapes=[pltpu.VMEM((LANES, width, LANES), f32)],
        compiler_params=PARAMS,
        name="transform",
    )(panel, signs.reshape(LANES, LANES))


def spread_lanes(parts, width):
    rolled = LANES // width if 8 * width > LANES else 0
    return pl.pallas_call(
        functools.partial(table_kernel, width, rolled),
        out_shape=jax.ShapeDtypeStruct((LANES * LANES, LANES), f32),
        in_specs=[VMEM],
        out_specs=VMEM,
        compiler_params=PARAMS,
        name="table",
    )(parts)


def reverse(i, bits):
    return int(format(i, f"0{bits}b")[::-1], 2) if bits else 0


def body(panel, signs, offsets, owners):
    width, row_count = panel.shape
    devices = lax.axis_size("row")
    bits = devices.bit_length() - 1
    count = offsets.shape[0]
    group = LANES // width
    per = count // group
    near = min(bits, 2)
    listed = [offsets]
    for t in range(1, 1 << near):
        listed.append(swapped(offsets, "row", t))
    parts = transform(panel, signs)
    arrays, entries = list(listed), [(t, 0) for t in range(1 << near)]
    if bits > near:
        far = jnp.concatenate(listed)
        far = swapped(far, "row", 1 << near)
        arrays.append(far)
        entries += [(len(arrays) - 1, t * count) for t in range(1 << near)]
        for level in range(near + 1, bits):
            held = jnp.concatenate([arrays[k][at : at + count] for k, at in entries])
            arrays.append(swapped(held, "row", 1 << level))
            entries += [(len(arrays) - 1, t * count) for t in range(1 << level)]
    table = spread_lanes(parts, width)

    def pick(*pieces):
        used = sorted({entries[t][0] for slots, _, _ in pieces for t in slots})
        full = [
            ([(t, used.index(entries[t][0]), entries[t][1]) for t in slots], first, rows)
            for slots, first, rows in pieces
        ]
        straight = sum(len(slots) * rows for slots, _, rows in pieces) * group <= 4096
        return pl.pallas_call(
            functools.partial(pick_kernel, width, full, count, straight),
            out_shape=[jax.ShapeDtypeStruct((len(slots) * rows, LANES), f32) for slots, _, rows in pieces],
            in_specs=[SMEM] * len(used) + [VMEM],
            out_specs=[VMEM] * len(pieces),
            compiler_params=PARAMS,
            name="pick",
        )(*[arrays[k] for k in used], table)

    def split(slots, levels):
        slots = sorted(slots, key=lambda t: [t >> level & 1 for level in levels])
        return slots[: len(slots) // 2], slots[len(slots) // 2 :]

    levels = list(range(bits - 1))
    half = per // 2
    keep_up, send_up = split(range(devices // 2, devices), levels)
    keep_low, send_low = split(range(devices // 2), levels)
    sent, kept = [None] * 3, [None] * 3
    sent[0], sent[1] = pick((send_up, 0, half), (send_up, half, half))
    sent[2], kept[0], kept[1] = pick((send_low, 0, per), (keep_up, 0, half), (keep_up, half, half))
    (kept[2],) = pick((keep_low, 0, per))
    totals = []
    for k in range(3):
        total, out = kept[k], sent[k]
        for step, level in enumerate(levels):
            if step:
                middle = total.shape[0] // 2
                total, out = total[:middle], total[middle:]
            other = swapped(out, "row", 1 << level)
            total = total + other
        totals.append(total)
    col_size = lax.axis_size("col")
    col_bits = col_size.bit_length() - 1
    own, other = [], []
    for part in range(2):
        mine = totals[2][part * per // 2 : (part + 1) * per // 2]
        if part:
            mine, own[0] = lax.optimization_barrier((mine, own[0]))
        own.append(mine + swapped(totals[part], "row", devices // 2))
        other.append(swapped(own[part], "col", col_size // 2))
    stacked = jnp.stack([jnp.concatenate(own), jnp.concatenate(other)])
    for level in reversed(range(col_bits - 1)):
        stacked = jnp.concatenate([stacked, swapped(stacked, "col", 1 << level)], axis=0)
    packed = [stacked[reverse(u, col_bits)] for u in range(group)]
    scale = 1.0 / (devices * row_count * count)
    gram = pl.pallas_call(
        functools.partial(gram_kernel, width, count, devices, scale),
        out_shape=jax.ShapeDtypeStruct((devices * width, LANES), f32),
        in_specs=[VMEM] * (1 + group),
        out_specs=VMEM,
        compiler_params=PARAMS,
        name="gram",
    )(owners, *packed)
    gram = gram.reshape(1 << near, devices >> near, width, LANES)
    total = gram[0]
    for t in range(1, 1 << near):
        total = total + swapped(gram[t], "row", t)
    for level in reversed(range(near, bits)):
        middle = total.shape[0] // 2
        total = total[:middle] + swapped(total[middle:], "row", 1 << level)
    return total


def solution(mesh):
    placed = (P("col", "row"), P("row"), P("row"), P("row", None))
    return jax.shard_map(body, mesh=mesh, in_specs=placed, out_specs=P("row", "col", None), check_vma=False)
```

```python
import functools

import jax
import jax.numpy as jnp
from jax import lax
from jax.experimental import pallas as pl
from jax.experimental.pallas import tpu as pltpu
from jax.sharding import PartitionSpec as P


LANES = 128
f32, bf16 = jnp.float32, jnp.bfloat16


def swapped(x, axis, distance):
    return lax.ppermute(x, axis, [(i, i ^ distance) for i in range(lax.axis_size(axis))])


def parity(v):
    v = v ^ (v >> 8)
    v = v ^ (v >> 4)
    v = v ^ (v >> 2)
    v = v ^ (v >> 1)
    return v & 1


def butterflies(values):
    step = 1
    while step < len(values):
        out = list(values)
        for i in range(len(values)):
            if not i & step:
                out[i] = values[i] + values[i | step]
                out[i | step] = values[i] - values[i | step]
        values = out
        step *= 2
    return values


def halves(x):
    top = x.astype(bf16)
    return top, (x - top.astype(f32)).astype(bf16)


def signs_of(rows, columns):
    row = lax.broadcasted_iota(jnp.int32, (rows, columns), 0)
    column = lax.broadcasted_iota(jnp.int32, (rows, columns), 1)
    return (1 - 2 * parity(row & (column & (LANES - 1)))).astype(f32).astype(bf16)


def times(hadamard, both):
    return lax.dot_general(hadamard, both, (((1,), (1,)), ((), ())), preferred_element_type=f32)


def transform_kernel(width, rolled, x_ref, sign_ref, part_ref, work_ref):
    bands = width // 8

    def first(lo, _):
        signs = [sign_ref[pl.ds(hi * 8 + lo, 1), :].astype(f32) for hi in range(16)]
        for band in range(bands):
            rows = pl.ds(band * 8, 8)
            values = []
            for hi in range(16):
                start = pl.multiple_of((hi * 8 + lo) * LANES, LANES)
                values.append(x_ref[rows, pl.ds(start, LANES)] * signs[hi])
            for hi, value in enumerate(butterflies(values)):
                work_ref[hi * 8 + lo, rows, :] = value
        return 0

    lax.fori_loop(0, 8, first, 0)
    hadamard = signs_of(LANES, 2 * LANES)
    straight = (8 - rolled) * width

    def second(hi, _):
        rows = [
            butterflies([work_ref[hi * 8 + lo, pl.ds(band * 8, 8), :] for lo in range(8)]) for band in range(bands)
        ]
        y = jnp.concatenate([rows[band][lo] for lo in range(8) for band in range(bands)], axis=0)
        top = pl.multiple_of(hi * 8 * width, LANES)
        part_ref[pl.ds(top, straight), :] = y[:straight]
        if rolled:
            both = jnp.concatenate(halves(y[straight:]), axis=1)
            part_ref[pl.ds(top + straight, LANES), :] = times(hadamard, both)
        return 0

    lax.fori_loop(0, 16, second, 0, unroll=4)


def table_kernel(width, rolled, part_ref, table_ref):
    group = LANES // width
    lane = lax.broadcasted_iota(jnp.int32, (LANES, LANES), 1) // width
    in_lane = [lane == g for g in range(group)]
    hadamard = signs_of(LANES, 2 * LANES)

    def some(hi, _):
        top = pl.multiple_of(hi * 8 * width, LANES)
        results = []
        for e in range(0, 8 - rolled, 2):
            rows = [
                jnp.concatenate(halves(part_ref[pl.ds(top + (e + i) * width, width), :]), axis=1) for i in range(2)
            ]
            mixed = times(hadamard, jnp.concatenate([row for row in rows for _ in range(group)], axis=0))
            results += [mixed[:, :LANES], mixed[:, LANES:]]
        if rolled:
            mixed = part_ref[pl.ds(top + (8 - rolled) * width, LANES), :]
            turned = [mixed] + [pltpu.roll(mixed, k * width, 1) for k in range(1, group)]
            for e in range(group):
                total = turned[-e % group]
                for g in range(1, group):
                    total = jnp.where(in_lane[g], turned[(g - e) % group], total)
                results.append(total)
        for e, result in enumerate(results):
            table_ref[pl.ds(pl.multiple_of((hi * 8 + e) * LANES, LANES), LANES), :] = result
        return 0

    lax.fori_loop(0, 16, some, 0, unroll=8)


def pick_kernel(width, pieces, count, straight, *refs):
    offset_refs, table_ref, out_refs = refs[: -1 - len(pieces)], refs[-1 - len(pieces)], refs[-len(pieces) :]
    group = LANES // width
    per = count // group
    lane = lax.broadcasted_iota(jnp.int32, (8, LANES), 1) // width
    sub = lax.broadcasted_iota(jnp.int32, (8, LANES), 0)
    in_sub = [sub == s for s in range(8)]
    in_lane = [lane == g for g in range(group)]
    me = lax.axis_index("row")
    for out_ref, (slots, first, rows) in zip(out_refs, pieces):
        for place, (slot, which, base) in enumerate(slots):
            sign = (1 - 2 * parity(me & (me ^ slot))).astype(f32)

            def block(inner):
                total = None
                for g in range(group):
                    part = None
                    for s in range(8):
                        spot = offset_refs[which][inner + (base + first + g * per + s)]
                        value = jnp.broadcast_to(table_ref[pl.ds(spot, 1), :], (8, LANES))
                        part = value if part is None else jnp.where(in_sub[s], value, part)
                    total = part if total is None else jnp.where(in_lane[g], part, total)
                return total * sign

            if straight:
                for inner in range(0, rows, 8):
                    out_ref[pl.ds(place * rows + inner, 8), :] = block(inner)
            else:

                def some(it, _):
                    inner = pl.multiple_of(it * 8, 8)
                    out_ref[pl.ds(place * rows + inner, 8), :] = block(inner)
                    return 0

                lax.fori_loop(0, rows // 8, some, 0)


def gram_kernel(width, count, named, scale, owner_ref, *refs):
    group = LANES // width
    per = count // group
    packed, out_ref = refs[:-1], refs[-1]
    lane = lax.broadcasted_iota(jnp.int32, (per, LANES), 1)
    in_lane = [lane // width == u for u in range(group)]
    turned = [[ref[...]] + [pltpu.roll(ref[...], k * width, 1) for k in range(1, group)] for ref in packed]
    parts, repeated = [], []
    for g in range(group):
        total, mine = turned[0][-g % group], turned[0][-g % group]
        for u in range(1, group):
            total = jnp.where(in_lane[u], turned[u][(u - g) % group], total)
            mine = jnp.where(in_lane[u], turned[0][(u - g) % group], mine)
        parts.append(total)
        repeated.append(mine)
    sketch = jnp.concatenate(parts, axis=0)
    mine = jnp.concatenate(repeated, axis=0)
    top, low = halves(sketch)
    mine_top, mine_low = halves(mine)
    whose = jnp.broadcast_to(owner_ref[...], (count, LANES))
    tall = lax.broadcasted_iota(jnp.int32, (count, LANES), 1) // width
    zero = jnp.zeros((count, LANES), bf16)
    me, col = lax.axis_index("row"), lax.axis_index("col")
    turned = lax.broadcasted_iota(jnp.int32, (LANES, LANES), 1) ^ (col * width)
    over = (((0,), (0,)), ((), ()))
    for block in range(named * width // LANES):
        match = whose == tall + block * group
        left = jnp.where(match, mine_top, zero)
        gram = lax.dot_general(left, top, over, preferred_element_type=f32)
        gram = gram + lax.dot_general(left, low, over, preferred_element_type=f32)
        left = jnp.where(match, mine_low, zero)
        gram = gram + lax.dot_general(left, top, over, preferred_element_type=f32)
        gram = jnp.take_along_axis(gram, turned, axis=1) * scale
        for k in range(group):
            slot = (block * group + k) ^ me
            place = (slot & 3) * (named // 4) + (slot >> 2)
            out_ref[pl.ds(pl.multiple_of(place * width, 8), width), :] = gram[k * width : (k + 1) * width]


VMEM = pl.BlockSpec(memory_space=pltpu.VMEM)
SMEM = pl.BlockSpec(memory_space=pltpu.SMEM)
PARAMS = pltpu.CompilerParams(vmem_limit_bytes=24 << 20)


def transform(panel, signs):
    width, _ = panel.shape
    rolled = LANES // width if 8 * width > LANES else 0
    return pl.pallas_call(
        functools.partial(transform_kernel, width, rolled),
        out_shape=jax.ShapeDtypeStruct((LANES * width, LANES), f32),
        in_specs=[VMEM] * 2,
        out_specs=VMEM,
        scratch_shapes=[pltpu.VMEM((LANES, width, LANES), f32)],
        compiler_params=PARAMS,
        name="transform",
    )(panel, signs.reshape(LANES, LANES))


def spread_lanes(parts, width):
    rolled = LANES // width if 8 * width > LANES else 0
    return pl.pallas_call(
        functools.partial(table_kernel, width, rolled),
        out_shape=jax.ShapeDtypeStruct((LANES * LANES, LANES), f32),
        in_specs=[VMEM],
        out_specs=VMEM,
        compiler_params=PARAMS,
        name="table",
    )(parts)


def reverse(i, bits):
    return int(format(i, f"0{bits}b")[::-1], 2) if bits else 0


def body(panel, signs, offsets, owners):
    width, row_count = panel.shape
    devices = lax.axis_size("row")
    bits = devices.bit_length() - 1
    count = offsets.shape[0]
    group = LANES // width
    per = count // group
    near = min(bits, 2)
    listed = [offsets]
    for t in range(1, 1 << near):
        listed.append(swapped(offsets, "row", t))
    parts = transform(panel, signs)
    arrays, entries = list(listed), [(t, 0) for t in range(1 << near)]
    if bits > near:
        far = jnp.concatenate(listed)
        far = swapped(far, "row", 1 << near)
        arrays.append(far)
        entries += [(len(arrays) - 1, t * count) for t in range(1 << near)]
        for level in range(near + 1, bits):
            held = jnp.concatenate([arrays[k][at : at + count] for k, at in entries])
            arrays.append(swapped(held, "row", 1 << level))
            entries += [(len(arrays) - 1, t * count) for t in range(1 << level)]
    table = spread_lanes(parts, width)

    def pick(*pieces):
        used = sorted({entries[t][0] for slots, _, _ in pieces for t in slots})
        full = [
            ([(t, used.index(entries[t][0]), entries[t][1]) for t in slots], first, rows)
            for slots, first, rows in pieces
        ]
        straight = sum(len(slots) * rows for slots, _, rows in pieces) * group <= 4096
        return pl.pallas_call(
            functools.partial(pick_kernel, width, full, count, straight),
            out_shape=[jax.ShapeDtypeStruct((len(slots) * rows, LANES), f32) for slots, _, rows in pieces],
            in_specs=[SMEM] * len(used) + [VMEM],
            out_specs=[VMEM] * len(pieces),
            compiler_params=PARAMS,
            name="pick",
        )(*[arrays[k] for k in used], table)

    def split(slots, levels):
        slots = sorted(slots, key=lambda t: [t >> level & 1 for level in levels])
        return slots[: len(slots) // 2], slots[len(slots) // 2 :]

    levels = list(range(bits - 1))
    half = per // 2
    keep_up, send_up = split(range(devices // 2, devices), levels)
    keep_low, send_low = split(range(devices // 2), levels)
    sent, kept = [None] * 3, [None] * 3
    sent[0], sent[1] = pick((send_up, 0, half), (send_up, half, half))
    sent[2], kept[0], kept[1] = pick((send_low, 0, per), (keep_up, 0, half), (keep_up, half, half))
    (kept[2],) = pick((keep_low, 0, per))
    totals = []
    for k in range(3):
        total, out = kept[k], sent[k]
        for step, level in enumerate(levels):
            if step:
                middle = total.shape[0] // 2
                total, out = total[:middle], total[middle:]
            other = swapped(out, "row", 1 << level)
            total = total + other
        totals.append(total)
    col_size = lax.axis_size("col")
    col_bits = col_size.bit_length() - 1
    own, other = [], []
    for part in range(2):
        mine = totals[2][part * per // 2 : (part + 1) * per // 2]
        if part:
            mine, own[0] = lax.optimization_barrier((mine, own[0]))
        own.append(mine + swapped(totals[part], "row", devices // 2))
        other.append(swapped(own[part], "col", col_size // 2))
    stacked = jnp.stack([jnp.concatenate(own), jnp.concatenate(other)])
    for level in reversed(range(col_bits - 1)):
        stacked = jnp.concatenate([stacked, swapped(stacked, "col", 1 << level)], axis=0)
    packed = [stacked[reverse(u, col_bits)] for u in range(group)]
    scale = 1.0 / (devices * row_count * count)
    gram = pl.pallas_call(
        functools.partial(gram_kernel, width, count, devices, scale),
        out_shape=jax.ShapeDtypeStruct((devices * width, LANES), f32),
        in_specs=[VMEM] * (1 + group),
        out_specs=VMEM,
        compiler_params=PARAMS,
        name="gram",
    )(owners, *packed)
    gram = gram.reshape(1 << near, devices >> near, width, LANES)
    total = gram[0]
    for t in range(1, 1 << near):
        total = total + swapped(gram[t], "row", t)
    for level in reversed(range(near, bits)):
        middle = total.shape[0] // 2
        total = total[:middle] + swapped(total[middle:], "row", 1 << level)
    return total


def solution(mesh):
    placed = (P("col", "row"), P("row"), P("row"), P("row", None))
    return jax.shard_map(body, mesh=mesh, in_specs=placed, out_specs=P("row", "col", None), check_vma=False)
```
